256 devices in a mesh: dp: 128 (over x, y, z_lo, core), sub: 2 (over z_hi).
Axes of the slice: x: 4, y: 4, z: 8 (z_hi: 2, z_lo: 4; z = z_hi * 4 + z_lo), core: 2. Of those that a mesh axis runs over, the one named last changes fastest.
Arguments:
- projections: float32 [49152, 128], P(('dp', 'sub')), may hold values from -6 to 6
- partner: int32 [49152], P(('dp', 'sub')), may hold values from 0 to 49151, as said below
Outputs:
- loss: float32 [], replicated
- grad_projections: float32 [49152, 128], P(('dp', 'sub'))
The draws below stay inside these ranges and needn't reach their ends.
Inputs may be any that keep to these rules, and one draw needn't show every extreme that they name: partner pairs the views: partner[partner[i]] = i and partner[i] != i for every view.
All inputs are finite; a program needn't handle non-finite values.
Results may differ from the reference program's by a relative error of at most 0.0003.
The reference program's roundings to bfloat16 on the way (of `unit_low` and `weight`) count: a program that leaves them out, or rounds other values in their place, can miss the bound.
Values may be sent and summed in bfloat16 or wider, within the bound.
No kernel may reach another device: no remote copies, remote signals or barrier semaphores. Data moves between devices by JAX's collectives and lax.ppermute only.
A program may use at most 128 MiB of HBM per device.

```python
import jax
import jax.numpy as jnp
from jax import lax

D = 128
V_DEV = 192
VIEWS = 49152
N_SUB = 2


def draw_partner(key, part):
    order = jax.random.permutation(key, VIEWS).astype(jnp.int32)
    pairs = order.reshape(VIEWS // 2, 2)
    result = jnp.zeros((VIEWS,), jnp.int32)
    result = result.at[pairs[:, 0]].set(pairs[:, 1])
    result = result.at[pairs[:, 1]].set(pairs[:, 0])
    return result


def steps_of(own_key, dims, split, low, largest):
    factor_of = 1.0
    for axis_at, blocks in split:
        steps = jax.random.uniform(jax.random.fold_in(jax.random.fold_in(own_key, 6), axis_at), (blocks,), jnp.float32, low / len(split), largest / len(split))
        factor_of = factor_of * jnp.repeat(jnp.exp(steps), dims[axis_at] // blocks).reshape((-1,) + (1,) * (len(dims) - 1 - axis_at))
    return factor_of


def scatter_about(rng, extent, scale, limit, pieces=(), kind=jnp.bfloat16):
    entries = scale * jax.random.normal(rng, extent, jnp.float32)
    if pieces:
        entries = entries * steps_of(rng, extent, pieces, -0.22, 0.18)
    return jnp.clip(entries, -limit, limit).astype(kind)


def setup_inputs(seed: int = 0) -> dict:
    streams_of = jax.random.split(jax.random.key(seed), 3)
    projections = scatter_about(streams_of[0], (VIEWS, D), 1.0, 6.0, ((0, 256),), jnp.float32)
    partner = draw_partner(jax.random.fold_in(streams_of[2], 71), 0)
    return {"projections": projections, "partner": partner}


TAU = 0.1
SHIFT = 10.0

def reference(projections, partner):
    inverse = lax.rsqrt(lax.optimization_barrier(jnp.sum(projections * projections, axis=1)) + 1e-06)
    unit = projections * inverse[:, None]
    unit_low = unit.astype(jnp.bfloat16)
    block = V_DEV * N_SUB
    count = VIEWS // block
    columns = jnp.arange(VIEWS, dtype=jnp.int32)

    def scores_of(index):
        start = (index * block).astype(jnp.int32)
        rows_low = lax.dynamic_slice_in_dim(unit_low, start, block, 0)
        score = jnp.dot(rows_low, unit_low.T, preferred_element_type=jnp.float32) / TAU
        rows = start + jnp.arange(block, dtype=jnp.int32)
        diag = columns[None, :] == rows[:, None]
        mates = lax.dynamic_slice_in_dim(partner, start, block, 0)
        hit = columns[None, :] == mates[:, None]
        return (score, diag, hit)

    def forward(index):
        score, diag, hit = scores_of(index)
        total = lax.optimization_barrier(jnp.sum(jnp.where(diag, 0.0, jnp.exp(score - SHIFT)), axis=1))
        lse = jnp.log(total) + SHIFT
        pos = lax.optimization_barrier(jnp.sum(jnp.where(hit, score, 0.0), axis=1))
        return (lse, lse - pos)
    lse, row_loss = lax.map(forward, jnp.arange(count, dtype=jnp.int32))
    lse = lse.reshape(VIEWS)
    row_loss = row_loss.reshape(VIEWS)
    loss = jnp.sum(row_loss) / VIEWS

    def backward(index):
        score, diag, hit = scores_of(index)
        start = (index * block).astype(jnp.int32)
        lse_rows = lax.dynamic_slice_in_dim(lse, start, block, 0)
        weight = jnp.exp(score - lse_rows[:, None]) + jnp.exp(score - lse[None, :])
        weight = weight - 2.0 * hit.astype(jnp.float32)
        weight = jnp.where(diag, 0.0, weight / TAU).astype(jnp.bfloat16)
        return jnp.dot(weight, unit_low, preferred_element_type=jnp.float32)
    grad_unit = lax.map(backward, jnp.arange(count, dtype=jnp.int32)).reshape(VIEWS, D)
    inner = lax.optimization_barrier(jnp.sum(unit * grad_unit, axis=1))
    grad = inverse[:, None] * (grad_unit - unit * inner[:, None])
    return (loss, grad)
```

```python
import jax
import jax.numpy as jnp
from jax import lax
from jax.experimental import pallas as pl
from jax.experimental.pallas import tpu as pltpu
from jax.sharding import Mesh
from jax.sharding import PartitionSpec as P

AXES = ("x", "y", "zl", "c", "zh")
XY = ("x", "y")
Z = ("zl", "zh")
EPS = 1e-06
LOG2E=1.4426950408889634
TAU=0.1
KS=LOG2E/TAU
SH=192; PADR=208; NB=16; NA=16; C=NA*SH; CH=256; NCH=C//CH

def col_bcast(row):
    return jnp.transpose(jnp.broadcast_to(row,(128,row.shape[1])))

def mates_of(rows_ref, sh):
    code = rows_ref[sh, SH:PADR, :].astype(jnp.float32)
    lo = code[2:4]*1.0
    m = code[0:2]*256.0 + code[2:4]
    a = col_bcast(m[0:1])
    b = col_bcast(m[1:2])[:SH-128]
    return jnp.concatenate([a,b],axis=0)

def k1_body(own_ref, rows_ref, cols_ref, colid_ref, trow_ref, tcol_ref, colsT, cacc, pacc, tr):
    for c in range(NCH):
        colsT[:, c*CH:(c+1)*CH] = jnp.transpose(cols_ref[c*CH:(c+1)*CH, :])
    cacc[...] = jnp.zeros_like(cacc); pacc[...] = jnp.zeros_like(pacc)
    b = own_ref[0]; own_off = own_ref[1]
    def shard(sh, masked):
        u = rows_ref[sh, 0:SH, :]
        mates = mates_of(rows_ref, sh)
        racc = jnp.zeros((SH,128), jnp.float32)
        for c in range(NCH):
            s = jnp.dot(u, colsT[:, c*CH:(c+1)*CH], preferred_element_type=jnp.float32)
            e = jnp.exp2(s*KS)
            if masked:
                cidx = lax.broadcasted_iota(jnp.int32,(SH,CH),1)+c*CH-own_off
                ridx = lax.broadcasted_iota(jnp.int32,(SH,CH),0)
                e = jnp.where(cidx==ridx, 0.0, e)
            racc = racc + e[:, :128] + e[:, 128:]
            cacc[:, c*CH:(c+1)*CH] += jnp.sum(e.reshape(SH//8,8,CH),axis=0)
            cid = colid_ref[c:c+1, :]
            h0 = jnp.where(mates==cid[:, :128], s[:, :128], 0.0)
            h1 = jnp.where(mates==cid[:, 128:], s[:, 128:], 0.0)
            pacc[...] += jnp.sum((h0+h1).reshape(SH//8,8,128),axis=0)
        t = jnp.sum(jnp.transpose(racc), axis=0, keepdims=True)
        tr[pl.ds(sh,1), 0:SH] = t
    tr[...] = jnp.ones_like(tr)
    shard(b, True)
    def step(k,_):
        shard((b+k) & (NB-1), False); return 0
    lax.fori_loop(1, NB, step, 0)
    for d in range(NB):
        trow_ref[d] = tr[...]
    tc=jnp.zeros((16,CH),jnp.float32)
    rows=[jnp.sum(cacc[:, c*CH:(c+1)*CH],axis=0,keepdims=True) for c in range(NCH)]
    ps=jnp.sum(pacc[...],axis=0,keepdims=True)
    rows.append(jnp.concatenate([ps,jnp.zeros_like(ps)],axis=1))
    rows.append(jnp.zeros((3,CH),jnp.float32))
    tc=jnp.concatenate(rows,axis=0)
    for d in range(tcol_ref.shape[0]):
        tcol_ref[d]=tc

def k1(own, rows, cols, colid, dup_c=NA):
    return pl.pallas_call(k1_body,
      out_shape=(jax.ShapeDtypeStruct((NB,16,256),jnp.float32),jax.ShapeDtypeStruct((dup_c,16,CH),jnp.float32)),
      in_specs=[pl.BlockSpec(memory_space=pltpu.SMEM)]+[pl.BlockSpec(memory_space=pltpu.VMEM)]*3,
      out_specs=(pl.BlockSpec(memory_space=pltpu.VMEM),)*2,
      scratch_shapes=[pltpu.VMEM((128,C),jnp.bfloat16),pltpu.VMEM((8,C),jnp.float32),pltpu.VMEM((8,128),jnp.float32),pltpu.VMEM((16,256),jnp.float32)],
      compiler_params=pltpu.CompilerParams(vmem_limit_bytes=40<<20))(own,rows,cols,colid)

def k2_body(own_ref, rows_ref, cols_ref, colid_ref, trow_ref, tcol_ref, g_ref, colsT, rrow, rcol):
    for c in range(NCH):
        colsT[:, c*CH:(c+1)*CH] = jnp.transpose(cols_ref[c*CH:(c+1)*CH, :])
    b = own_ref[0]; own_off = own_ref[1]
    T=trow_ref[0]
    for d in range(1,trow_ref.shape[0]): T=T+trow_ref[d]
    rrow[...]=(1.0/TAU)/T
    Tc=tcol_ref[0]
    for d in range(1,tcol_ref.shape[0]): Tc=Tc+tcol_ref[d]
    rid=lax.broadcasted_iota(jnp.int32,(16,CH),0)
    isT=rid<NCH
    Ts=jnp.where(isT,Tc,1.0)
    rcol[...]=(1.0/TAU)/Ts
    S=jnp.where(isT,jnp.log(Ts),jnp.where(rid==NCH,Tc*(-1.0/TAU),0.0))
    Sv=S[0:8]+S[8:16]
    Sv=Sv[:, :128]+Sv[:, 128:]
    for d in range(NB):
        g_ref[d, SH:SH+8, :]=Sv
    def shard(sh, masked):
        u = rows_ref[sh, 0:SH, :]
        mates = mates_of(rows_ref, sh)
        ri = col_bcast(rrow[pl.ds(sh,1), 0:SH])
        acc = jnp.zeros((SH,128), jnp.float32)
        for c in range(NCH):
            s = jnp.dot(u, colsT[:, c*CH:(c+1)*CH], preferred_element_type=jnp.float32)
            e = jnp.exp2(s*KS)
            cid = colid_ref[c:c+1, :]; rj=rcol[c:c+1, :]
            ws=[]
            for l in (0,128):
                w = e[:, l:l+128]*(ri+rj[:, l:l+128])
                w = jnp.where(mates==cid[:, l:l+128], w-2.0/TAU, w)
                if masked:
                    cidx = lax.broadcasted_iota(jnp.int32,(SH,128),1)+(c*CH+l)-own_off
                    ridx = lax.broadcasted_iota(jnp.int32,(SH,128),0)
                    w = jnp.where(cidx==ridx, 0.0, w)
                ws.append(w.astype(jnp.bfloat16))
            w=jnp.concatenate(ws,axis=1)
            acc = acc + jnp.dot(w, cols_ref[c*CH:(c+1)*CH, :], preferred_element_type=jnp.float32)
        g_ref[sh, 0:SH, :] = acc
    shard(b, True)
    def step(k,_):
        shard((b+k) & (NB-1), False); return 0
    lax.fori_loop(1, NB, step, 0)

def k2(own, rows, cols, colid, trow, tcol):
    return pl.pallas_call(k2_body,
      out_shape=jax.ShapeDtypeStruct((NB,SH+8,128),jnp.float32),
      in_specs=[pl.BlockSpec(memory_space=pltpu.SMEM)]+[pl.BlockSpec(memory_space=pltpu.VMEM)]*5,
      out_specs=pl.BlockSpec(memory_space=pltpu.VMEM),
      scratch_shapes=[pltpu.VMEM((128,C),jnp.bfloat16),pltpu.VMEM((16,256),jnp.float32),pltpu.VMEM((16,CH),jnp.float32)],
      compiler_params=pltpu.CompilerParams(vmem_limit_bytes=40<<20))(own,rows,cols,colid,trow,tcol)


def inverse_norm(p):
    return lax.rsqrt(jnp.sum(p * p, axis=1, keepdims=True) + EPS)


def prep_body(p_ref, mate_ref, pay_ref, zpay_ref):
    p = p_ref[...]
    low = (p * inverse_norm(p)).astype(jnp.bfloat16)
    m = mate_ref[...]
    hi = (m >> 8).astype(jnp.float32)
    lo = (m & 255).astype(jnp.float32)
    code = jnp.concatenate([hi, lo, jnp.zeros((12, 128), jnp.float32)], axis=0).astype(jnp.bfloat16)
    for d in range(pay_ref.shape[0]):
        pay_ref[d, 0:SH, :] = low
        pay_ref[d, SH:PADR, :] = code
    for d in range(zpay_ref.shape[0]):
        zpay_ref[d] = low


def prep(p, mate):
    return pl.pallas_call(
        prep_body,
        out_shape=(
            jax.ShapeDtypeStruct((NB, PADR, 128), jnp.bfloat16),
            jax.ShapeDtypeStruct((8, SH, 128), jnp.bfloat16),
        ),
        in_specs=[pl.BlockSpec(memory_space=pltpu.VMEM)] * 2,
        out_specs=(pl.BlockSpec(memory_space=pltpu.VMEM),) * 2,
    )(p, mate)


def final_body(p_ref, g_ref, loss_ref, grad_ref):
    p = p_ref[...]
    inv = inverse_norm(p)
    unit = p * inv
    g = g_ref[0]
    for d in range(1, NB):
        g = g + g_ref[d]
    loss_ref[0, 0] = jnp.sum(g[SH:]) / (NA * NB * SH)
    gu = g[:SH]
    inner = jnp.sum(unit * gu, axis=1, keepdims=True)
    grad_ref[...] = inv * (gu - unit * inner)


def final(p, g):
    return pl.pallas_call(
        final_body,
        out_shape=(
            jax.ShapeDtypeStruct((1, 1), jnp.float32),
            jax.ShapeDtypeStruct((SH, 128), jnp.float32),
        ),
        in_specs=[pl.BlockSpec(memory_space=pltpu.VMEM)] * 2,
        out_specs=(pl.BlockSpec(memory_space=pltpu.SMEM), pl.BlockSpec(memory_space=pltpu.VMEM)),
    )(p, g)


def body(projections, partner):
    xy = lax.axis_index(XY)
    own_a = lax.axis_index(("c", "zl", "zh"))
    mate = jnp.pad(partner, (0, 64)).reshape(2, 128)
    pay, zpay = prep(projections, mate)
    rows = lax.all_to_all(pay, XY, 0, 0)
    zg = lax.all_to_all(zpay, Z, 0, 0)
    cols = lax.all_gather(zg, "c").reshape(C, 128)
    own = jnp.stack([xy, own_a * SH]).astype(jnp.int32)
    p = jnp.arange(16 * CH, dtype=jnp.int32)
    k = p // SH
    shard = ((k % 8) // 2) * 4 + (k // 8) * 2 + k % 2
    colid = ((xy * NA + shard) * SH + p % SH).astype(jnp.float32).reshape(16, CH)
    trow, tcol = k1(own, rows, cols, colid)
    trow = lax.all_to_all(trow, XY, 0, 0)
    tcol = lax.all_to_all(tcol, ("zl", "c", "zh"), 0, 0)
    g = k2(own, rows, cols, colid, trow, tcol)
    g = lax.all_to_all(g, XY, 0, 0)
    loss, grad = final(projections, g)
    return (loss[0, 0], grad)


def solution(mesh):
    finer = Mesh(mesh.devices.reshape(4, 4, 4, 2, mesh.shape["sub"]), AXES)
    in_specs = (P(AXES, None), P(AXES))
    out_specs = (P(), P(AXES, None))
    return jax.shard_map(body, mesh=finer, in_specs=in_specs, out_specs=out_specs, check_vma=False)
```

```python
import jax
import jax.numpy as jnp
from jax import lax
from jax.experimental import pallas as pl
from jax.experimental.pallas import tpu as pltpu
from jax.sharding import Mesh
from jax.sharding import PartitionSpec as P

AXES = ("x", "y", "zl", "c", "zh")
XY = ("x", "y")
ZC = ("zl", "c", "zh")
NZ = 8
EPS = 1e-06
LOG2E=1.4426950408889634
TAU=0.1
KS=LOG2E/TAU
SH=192; PADR=208; NB=16; NA=16; C=NA*SH; CH=256; NCH=C//CH

def col_bcast(row):
    return jnp.transpose(jnp.broadcast_to(row,(128,row.shape[1])))

def mates_of(rows_ref, sh):
    code = rows_ref[sh, SH:PADR, :].astype(jnp.float32)
    lo = code[2:4]*1.0
    m = code[0:2]*256.0 + code[2:4]
    a = col_bcast(m[0:1])
    b = col_bcast(m[1:2])[:SH-128]
    return jnp.concatenate([a,b],axis=0)

def k1_body(own_ref, rows_ref, pair_ref, d1, d2, d3, s1, s2, s3, d4, s4, colid_ref, trow_ref, tcol_ref, cols_ref, colsT, cacc, pacc, tr):
    z = own_ref[2]
    core = own_ref[3]
    sg = 1 - 2 * core
    def put(at, piece):
        n = piece.shape[0]
        cols_ref[pl.ds(pl.multiple_of(at, SH), n), :] = piece
    for off, ref in ((0, pair_ref), (-1, d1), (-2, d2), (-3, d3), (1, s1), (2, s2), (3, s3)):
        zs = (z + off * sg + NZ) & (NZ - 1)
        put(zs * (2 * SH), ref[...].reshape(2 * SH, 128))
    z4 = ((z + 4) & (NZ - 1)) * (2 * SH)
    put(z4 + core * SH, d4[...])
    put(z4 + (1 - core) * SH, s4[...])
    for c in range(NCH):
        colsT[:, c*CH:(c+1)*CH] = jnp.transpose(cols_ref[c*CH:(c+1)*CH, :])
    cacc[...] = jnp.zeros_like(cacc); pacc[...] = jnp.zeros_like(pacc)
    b = own_ref[0]; own_off = own_ref[1]
    def shard(sh, masked):
        u = rows_ref[sh, 0:SH, :]
        mates = mates_of(rows_ref, sh)
        racc = jnp.zeros((SH,128), jnp.float32)
        for c in range(NCH):
            s = jnp.dot(u, colsT[:, c*CH:(c+1)*CH], preferred_element_type=jnp.float32)
            e = jnp.exp2(s*KS)
            if masked:
                cidx = lax.broadcasted_iota(jnp.int32,(SH,CH),1)+c*CH-own_off
                ridx = lax.broadcasted_iota(jnp.int32,(SH,CH),0)
                e = jnp.where(cidx==ridx, 0.0, e)
            racc = racc + e[:, :128] + e[:, 128:]
            cacc[:, c*CH:(c+1)*CH] += jnp.sum(e.reshape(SH//8,8,CH),axis=0)
            cid = colid_ref[c:c+1, :]
            h0 = jnp.where(mates==cid[:, :128], s[:, :128], 0.0)
            h1 = jnp.where(mates==cid[:, 128:], s[:, 128:], 0.0)
            pacc[...] += jnp.sum((h0+h1).reshape(SH//8,8,128),axis=0)
        t = jnp.sum(jnp.transpose(racc), axis=0, keepdims=True)
        tr[pl.ds(sh,1), 0:SH] = t
    tr[...] = jnp.ones_like(tr)
    shard(b, True)
    def step(k,_):
        shard((b+k) & (NB-1), False); return 0
    lax.fori_loop(1, NB, step, 0)
    for d in range(NB):
        trow_ref[d] = tr[...]
    tc=jnp.zeros((16,CH),jnp.float32)
    rows=[jnp.sum(cacc[:, c*CH:(c+1)*CH],axis=0,keepdims=True) for c in range(NCH)]
    ps=jnp.sum(pacc[...],axis=0,keepdims=True)
    rows.append(jnp.concatenate([ps,jnp.zeros_like(ps)],axis=1))
    rows.append(jnp.zeros((3,CH),jnp.float32))
    tc=jnp.concatenate(rows,axis=0)
    tcol_ref[...]=tc

def k1(own, rows, pieces, colid):
    return pl.pallas_call(
        k1_body,
        out_shape=(
            jax.ShapeDtypeStruct((NB, 16, 256), jnp.float32),
            jax.ShapeDtypeStruct((16, CH), jnp.float32),
            jax.ShapeDtypeStruct((C, 128), jnp.bfloat16),
        ),
        in_specs=[pl.BlockSpec(memory_space=pltpu.SMEM)] + [pl.BlockSpec(memory_space=pltpu.VMEM)] * (2 + len(pieces)),
        out_specs=(pl.BlockSpec(memory_space=pltpu.VMEM),) * 3,
        scratch_shapes=[
            pltpu.VMEM((128, C), jnp.bfloat16),
            pltpu.VMEM((8, C), jnp.float32),
            pltpu.VMEM((8, 128), jnp.float32),
            pltpu.VMEM((16, 256), jnp.float32),
        ],
        compiler_params=pltpu.CompilerParams(vmem_limit_bytes=40 << 20),
    )(own, rows, *pieces, colid)


def k2_body(own_ref, rows_ref, cols_ref, colid_ref, trow_ref, t0, t1, t2, g_ref, colsT, rrow, rcol):
    tc_refs = (t0, t1, t2)
    for c in range(NCH):
        colsT[:, c*CH:(c+1)*CH] = jnp.transpose(cols_ref[c*CH:(c+1)*CH, :])
    b = own_ref[0]; own_off = own_ref[1]
    T=trow_ref[0]
    for d in range(1,trow_ref.shape[0]): T=T+trow_ref[d]
    rrow[...]=(1.0/TAU)/T
    Tc=tc_refs[0][...]+tc_refs[1][...]+tc_refs[2][...]
    rid=lax.broadcasted_iota(jnp.int32,(16,CH),0)
    isT=rid<NCH
    Ts=jnp.where(isT,Tc,1.0)
    rcol[...]=(1.0/TAU)/Ts
    S=jnp.where(isT,jnp.log(Ts),jnp.where(rid==NCH,Tc*(-1.0/TAU),0.0))
    Sv=S[0:8]+S[8:16]
    Sv=Sv[:, :128]+Sv[:, 128:]
    for d in range(NB):
        g_ref[d, SH:SH+8, :]=Sv
    def shard(sh, masked):
        u = rows_ref[sh, 0:SH, :]
        mates = mates_of(rows_ref, sh)
        ri = col_bcast(rrow[pl.ds(sh,1), 0:SH])
        acc = jnp.zeros((SH,128), jnp.float32)
        for c in range(NCH):
            s = jnp.dot(u, colsT[:, c*CH:(c+1)*CH], preferred_element_type=jnp.float32)
            e = jnp.exp2(s*KS)
            cid = colid_ref[c:c+1, :]; rj=rcol[c:c+1, :]
            ws=[]
            for l in (0,128):
                w = e[:, l:l+128]*(ri+rj[:, l:l+128])
                w = jnp.where(mates==cid[:, l:l+128], w-2.0/TAU, w)
                if masked:
                    cidx = lax.broadcasted_iota(jnp.int32,(SH,128),1)+(c*CH+l)-own_off
                    ridx = lax.broadcasted_iota(jnp.int32,(SH,128),0)
                    w = jnp.where(cidx==ridx, 0.0, w)
                ws.append(w.astype(jnp.bfloat16))
            w=jnp.concatenate(ws,axis=1)
            acc = acc + jnp.dot(w, cols_ref[c*CH:(c+1)*CH, :], preferred_element_type=jnp.float32)
        g_ref[sh, 0:SH, :] = acc
    shard(b, True)
    def step(k,_):
        shard((b+k) & (NB-1), False); return 0
    lax.fori_loop(1, NB, step, 0)

def k2(own, rows, cols, colid, trow, tcol):
    return pl.pallas_call(k2_body,
      out_shape=jax.ShapeDtypeStruct((NB,SH+8,128),jnp.float32),
      in_specs=[pl.BlockSpec(memory_space=pltpu.SMEM)]+[pl.BlockSpec(memory_space=pltpu.VMEM)]*7,
      out_specs=pl.BlockSpec(memory_space=pltpu.VMEM),
      scratch_shapes=[pltpu.VMEM((128,C),jnp.bfloat16),pltpu.VMEM((16,256),jnp.float32),pltpu.VMEM((16,CH),jnp.float32)],
      compiler_params=pltpu.CompilerParams(vmem_limit_bytes=40<<20))(own,rows,cols,colid,trow,*tcol)


def inverse_norm(p):
    return lax.rsqrt(jnp.sum(p * p, axis=1, keepdims=True) + EPS)


def prep_body(core_ref, p_ref, q_ref, mate_ref, pay_ref, pair_ref, low_ref):
    core = core_ref[0]
    p = p_ref[...]
    low = (p * inverse_norm(p)).astype(jnp.bfloat16)
    q = q_ref[...]
    other = (q * inverse_norm(q)).astype(jnp.bfloat16)
    m = mate_ref[...]
    hi = (m >> 8).astype(jnp.float32)
    lo = (m & 255).astype(jnp.float32)
    code = jnp.concatenate([hi, lo, jnp.zeros((12, 128), jnp.float32)], axis=0).astype(jnp.bfloat16)
    for d in range(pay_ref.shape[0]):
        pay_ref[d, 0:SH, :] = low
        pay_ref[d, SH:PADR, :] = code
    pair_ref[core] = low
    pair_ref[1 - core] = other
    low_ref[...] = low


def prep(core, p, q, mate):
    return pl.pallas_call(
        prep_body,
        out_shape=(
            jax.ShapeDtypeStruct((NB, PADR, 128), jnp.bfloat16),
            jax.ShapeDtypeStruct((2, SH, 128), jnp.bfloat16),
            jax.ShapeDtypeStruct((SH, 128), jnp.bfloat16),
        ),
        in_specs=[pl.BlockSpec(memory_space=pltpu.SMEM)] + [pl.BlockSpec(memory_space=pltpu.VMEM)] * 3,
        out_specs=(pl.BlockSpec(memory_space=pltpu.VMEM),) * 3,
    )(core, p, q, mate)


def final_body(p_ref, g_ref, loss_ref, grad_ref):
    p = p_ref[...]
    inv = inverse_norm(p)
    unit = p * inv
    g = g_ref[0]
    for d in range(1, NB):
        g = g + g_ref[d]
    loss_ref[0, 0] = jnp.sum(g[SH:]) / (NA * NB * SH)
    gu = g[:SH]
    inner = jnp.sum(unit * gu, axis=1, keepdims=True)
    grad_ref[...] = inv * (gu - unit * inner)


def final(p, g):
    return pl.pallas_call(
        final_body,
        out_shape=(
            jax.ShapeDtypeStruct((1, 1), jnp.float32),
            jax.ShapeDtypeStruct((SH, 128), jnp.float32),
        ),
        in_specs=[pl.BlockSpec(memory_space=pltpu.VMEM)] * 2,
        out_specs=(pl.BlockSpec(memory_space=pltpu.SMEM), pl.BlockSpec(memory_space=pltpu.VMEM)),
    )(p, g)


def swap(value):
    return lax.ppermute(value, "c", [(0, 1), (1, 0)])


def seat(z, core):
    z = z % NZ
    return ((z % 4) * 2 + core) * 2 + z // 4


def along_z(value, k):
    pairs = []
    for z in range(NZ):
        pairs.append((seat(z, 0), seat(z + k, 0)))
        pairs.append((seat(z, 1), seat(z - k, 1)))
    return lax.ppermute(value, ZC, pairs)


def body(projections, partner):
    xy = lax.axis_index(XY)
    z = lax.axis_index(("zh", "zl"))
    core = lax.axis_index("c")
    own = jnp.stack([xy, (2 * z + core) * SH, z, core]).astype(jnp.int32)
    mate = jnp.pad(partner, (0, 64)).reshape(2, 128)
    pay, pair, low = prep(own[3:], projections, swap(projections), mate)
    rows = lax.all_to_all(pay, XY, 0, 0)
    direct = [along_z(pair, k) for k in (1, 2, 3)] + [along_z(low, 4)]
    crossed = [swap(piece) for piece in direct]
    pieces = [pair, *direct[:3], *crossed[:3], direct[3], crossed[3]]
    p = jnp.arange(16 * CH, dtype=jnp.int32)
    zp = p // (2 * SH)
    shard = (zp % 4) * 4 + (p // SH % 2) * 2 + zp // 4
    colid = ((xy * NA + shard) * SH + p % SH).astype(jnp.float32).reshape(16, CH)
    trow, tcol, cols = k1(own, rows, pieces, colid)
    trow = lax.all_to_all(trow, XY, 0, 0)
    chip = tcol + swap(tcol)
    far = [along_z(chip, k) for k in (1, 2, 3)]
    far.append(lax.ppermute(chip, ZC, [(seat(z, 0), seat(z + 4, 0)) for z in range(NZ)]))
    part = (far[0] + far[1]) + (far[2] + far[3])
    g = k2(own, rows, cols, colid, trow, (chip, part, swap(part)))
    g = lax.all_to_all(g, XY, 0, 0)
    loss, grad = final(projections, g)
    return (loss[0, 0], grad)


def solution(mesh):
    finer = Mesh(mesh.devices.reshape(4, 4, 4, 2, mesh.shape["sub"]), AXES)
    in_specs = (P(AXES, None), P(AXES))
    out_specs = (P(), P(AXES, None))
    return jax.shard_map(body, mesh=finer, in_specs=in_specs, out_specs=out_specs, check_vma=False)
```

```python
import jax
import jax.numpy as jnp
from jax import lax
from jax.experimental import pallas as pl
from jax.experimental.pallas import tpu as pltpu
from jax.sharding import Mesh
from jax.sharding import PartitionSpec as P

AXES = ("x", "y", "zl", "c", "zh")
XY = ("x", "y")
ZC = ("zl", "c", "zh")
EPS = 1e-06
NZ = 8
LOG2E = 1.4426950408889634
TAU = 0.1
KS = LOG2E / TAU
SH = 192
PADR = 208
NB = 16
NA = 16
C = NA * SH
R = NB * SH
CH = 256
T1 = 1536
N1 = R // T1
PER1 = T1 // SH
T2 = 768
N2 = R // T2
PER2 = T2 // SH
NCH = C // CH
SUB = 64
CW = 256
NW = C // CW


def col_bcast(row):
    return jnp.transpose(jnp.broadcast_to(row, (128, row.shape[1])))


def load_rows(rows_ref, rows, mates, s):
    rows[pl.ds(s * SH, SH), :] = rows_ref[s, 0:SH, :]
    code = rows_ref[s, SH:PADR, :]
    code = code.astype(jnp.float32)
    m = code[0:2] * 256.0 + code[2:4]
    mates[pl.ds(s * SH, 128), :] = col_bcast(m[0:1])
    mates[pl.ds(s * SH + 128, 64), :] = col_bcast(m[1:2])[: SH - 128]


def diag_rows(b, count):
    r = lax.broadcasted_iota(jnp.int32, (count, 128), 0) - (b % (count // SH)) * SH
    return jnp.where((r >= 0) & (r < SH), r, -100000)


def diag_of(rid, lane_at, core):
    lanes = lax.broadcasted_iota(jnp.int32, (1, 128), 1) + (lane_at - core * SH)
    return rid == lanes


def k1_body(own_ref, rows_ref, pair_ref, d1, d2, d3, s1, s2, s3, d4, s4, colid_ref,
            trow_ref, tcol_ref, cols_ref, rows_out, mates, rows, colsT, racc, hval, cacc, tr, sems):
    b = own_ref[0]
    z = own_ref[1]
    core = own_ref[2]

    places = [(pair_ref.at[0], core), (pair_ref.at[1], 1 - core), (d4, 8 + core), (s4, 9 - core)]
    for off, ref in ((-1, d1), (-2, d2), (-3, d3), (1, s1), (2, s2), (3, s3)):
        slot = jnp.where(core == 0, off & 7, (-off) & 7) * 2
        first = core if off < 0 else 1 - core
        places += [(ref.at[0], slot + first), (ref.at[1], slot + 1 - first)]
    copies = []
    for n, (piece, slot) in enumerate(places):
        to = cols_ref.at[pl.ds(pl.multiple_of(slot * SH, SH), SH), :]
        copies.append(pltpu.make_async_copy(piece, to, sems.at[n]))
    for copy in copies:
        copy.start()
    for q in range(NB):
        load_rows(rows_ref, rows, mates, q)
    for copy in copies:
        copy.wait()
    keep = pltpu.make_async_copy(rows, rows_out, sems.at[16])
    keep.start()
    for c in range(NCH):
        colsT[:, c * CH : (c + 1) * CH] = jnp.transpose(cols_ref[c * CH : (c + 1) * CH, :])
    cacc[...] = jnp.zeros_like(cacc)

    def tile(t, masked):
        at = pl.multiple_of(t * T1, T1)
        u = rows[pl.ds(at, T1), :]
        rid = diag_rows(b, T1) if masked else None
        for c in range(NW):
            s = jnp.dot(u, colsT[:, c * CW : (c + 1) * CW], preferred_element_type=jnp.float32)
            sums = [None] * (CW // 128)
            for r in range(0, T1, SUB):
                m = mates[pl.ds(pl.multiple_of(at + r, SUB), SUB), :]
                ra = None if c == 0 else racc[r : r + SUB, :]
                hv = jnp.zeros((SUB, 128), jnp.float32) if c == 0 else hval[r : r + SUB, :]
                for l in range(0, CW, 128):
                    p = c * CW + l
                    sl = s[r : r + SUB, l : l + 128]
                    el = jnp.exp2(sl * KS)
                    if masked and p < 2 * SH:
                        el = jnp.where(diag_of(rid[r : r + SUB], p, core), 0.0, el)
                    ra = el if ra is None else ra + el
                    hv = jnp.where(m == colid_ref[p // 256 : p // 256 + 1, p % 256 : p % 256 + 128], sl, hv)
                    cs = jnp.sum(el.reshape(SUB // 8, 8, 128), axis=0)
                    sums[l // 128] = cs if r == 0 else sums[l // 128] + cs
                racc[r : r + SUB, :] = ra
                hval[r : r + SUB, :] = hv
            for l in range(0, CW, 128):
                cacc[:, c * CW + l : c * CW + l + 128] += sums[l // 128]
        for q in range(PER1):
            part = jnp.sum(jnp.transpose(racc[q * SH : (q + 1) * SH, :]), axis=0, keepdims=True)
            tr[pl.ds(t * PER1 + q, 1), 0:SH] = part
        return jnp.sum(hval[...].reshape(T1 // 8, 8, 128), axis=0)

    tr[...] = jnp.ones_like(tr)
    own_tile = b // PER1
    pos = tile(own_tile, True)

    def step(k, pos):
        return pos + tile((own_tile + k) & (N1 - 1), False)

    pos = lax.fori_loop(1, N1, step, pos)
    copies = [pltpu.make_async_copy(tr, trow_ref.at[d], sems.at[d]) for d in range(NB)]
    for copy in copies:
        copy.start()
    tcol_ref[...] = jnp.zeros_like(tcol_ref)
    tcol_ref[8:16, 0:128] = pos
    total = jnp.sum(cacc[...], axis=0, keepdims=True)
    for k in range(NZ):
        tcol_ref[pl.ds((z + k) & 7, 1), :] = total[:, k * 2 * SH : (k + 1) * 2 * SH]
    for copy in copies:
        copy.wait()
    keep.wait()


def k1(own, rows, pieces, colid):
    return pl.pallas_call(
        k1_body,
        out_shape=(
            jax.ShapeDtypeStruct((NB, 16, 256), jnp.float32),
            jax.ShapeDtypeStruct((16, 2 * SH), jnp.float32),
            jax.ShapeDtypeStruct((C, 128), jnp.bfloat16),
            jax.ShapeDtypeStruct((R, 128), jnp.bfloat16),
            jax.ShapeDtypeStruct((R, 128), jnp.float32),
        ),
        in_specs=[pl.BlockSpec(memory_space=pltpu.SMEM), pl.BlockSpec(memory_space=pltpu.VMEM)]
        + [pl.BlockSpec(memory_space=pltpu.HBM)] * len(pieces)
        + [pl.BlockSpec(memory_space=pltpu.VMEM)],
        out_specs=(
            pl.BlockSpec(memory_space=pltpu.HBM),
            pl.BlockSpec(memory_space=pltpu.VMEM),
            pl.BlockSpec(memory_space=pltpu.VMEM),
            pl.BlockSpec(memory_space=pltpu.HBM),
            pl.BlockSpec(memory_space=pltpu.VMEM),
        ),
        scratch_shapes=[
            pltpu.VMEM((R, 128), jnp.bfloat16),
            pltpu.VMEM((128, C), jnp.bfloat16),
            pltpu.VMEM((T1, 128), jnp.float32),
            pltpu.VMEM((T1, 128), jnp.float32),
            pltpu.VMEM((8, C), jnp.float32),
            pltpu.VMEM((NB, 256), jnp.float32),
            pltpu.SemaphoreType.DMA((17,)),
        ],
        compiler_params=pltpu.CompilerParams(vmem_limit_bytes=12 << 20),
    )(own, rows, *pieces, colid)


def mid_body(trow_ref, f1, f2, f3, f4, ris_ref, part_ref):
    part_ref[...] = (f1[...] + f2[...]) + (f3[...] + f4[...])
    total = trow_ref[0]
    for d in range(1, NB):
        total = total + trow_ref[d]
    rrow = (1.0 / TAU) / total
    for q in range(NB):
        ris_ref[q * SH : (q + 1) * SH, :] = col_bcast(rrow[q : q + 1, 0:SH])


def mid(trow, far):
    return pl.pallas_call(
        mid_body,
        out_shape=(
            jax.ShapeDtypeStruct((R, 128), jnp.float32),
            jax.ShapeDtypeStruct((16, 2 * SH), jnp.float32),
        ),
        in_specs=[pl.BlockSpec(memory_space=pltpu.VMEM)] * 5,
        out_specs=(pl.BlockSpec(memory_space=pltpu.VMEM),) * 2,
        compiler_params=pltpu.CompilerParams(vmem_limit_bytes=6 << 20),
    )(trow, *far)


def k2_body(own_ref, rows_in, mates, ris, cols_ref, colid_ref, t0, t1, t2, g_ref, rows, colsT, rcol, sem):
    fetch = pltpu.make_async_copy(rows_in, rows, sem)
    fetch.start()
    b = own_ref[0]
    z = own_ref[1]
    core = own_ref[2]
    for c in range(NCH):
        colsT[:, c * CH : (c + 1) * CH] = jnp.transpose(cols_ref[c * CH : (c + 1) * CH, :])
    tc = t0[...] + t1[...] + t2[...]
    logs = jnp.sum(jnp.log(tc[0:8]), axis=0, keepdims=True)
    pos = jnp.sum(tc[8:16], axis=0, keepdims=True)
    loss = logs - pos * (1.0 / TAU)
    loss = loss[:, 0:128] + loss[:, 128:256] + loss[:, 256:384]
    loss = jnp.concatenate([loss, jnp.zeros((7, 128), jnp.float32)], axis=0)
    for d in range(NB):
        g_ref[d, SH : SH + 8, :] = loss
    tall = t0[0:8] + t1[0:8] + t2[0:8]
    rall = (1.0 / TAU) / tall
    rcol[8:16, :] = rall
    for k in range(NZ):
        rcol[k : k + 1, :] = rcol[pl.ds(8 + ((z + k) & 7), 1), :]

    def tile(t, masked):
        at = pl.multiple_of(t * T2, T2)
        u = rows[pl.ds(at, T2), :]
        rid = diag_rows(b, T2) if masked else None
        acc = jnp.zeros((T2, 128), jnp.float32)
        for c in range(NW):
            s = jnp.dot(u, colsT[:, c * CW : (c + 1) * CW], preferred_element_type=jnp.float32)
            blocks = []
            for r in range(0, T2, SUB):
                here = pl.ds(pl.multiple_of(at + r, SUB), SUB)
                m = mates[here, :]
                ri = ris[here, :]
                ws = []
                for l in range(0, CW, 128):
                    p = c * CW + l
                    rj = rcol[p // 384 : p // 384 + 1, p % 384 : p % 384 + 128]
                    w = jnp.exp2(s[r : r + SUB, l : l + 128] * KS) * (ri + rj)
                    w = jnp.where(m == colid_ref[p // 256 : p // 256 + 1, p % 256 : p % 256 + 128], w - 2.0 / TAU, w)
                    if masked and p < 2 * SH:
                        w = jnp.where(diag_of(rid[r : r + SUB], p, core), 0.0, w)
                    ws.append(w.astype(jnp.bfloat16))
                blocks.append(jnp.concatenate(ws, axis=1))
            w = jnp.concatenate(blocks, axis=0)
            acc = acc + jnp.dot(w, cols_ref[c * CW : (c + 1) * CW, :], preferred_element_type=jnp.float32)
        for q in range(PER2):
            g_ref[t * PER2 + q, 0:SH, :] = acc[q * SH : (q + 1) * SH]

    fetch.wait()
    own_tile = b // PER2
    tile(own_tile, True)

    def step(k, _):
        tile((own_tile + k) & (N2 - 1), False)
        return 0

    lax.fori_loop(1, N2, step, 0)


def k2(own, rows, mates, ris, cols, colid, tcol):
    return pl.pallas_call(
        k2_body,
        out_shape=jax.ShapeDtypeStruct((NB, SH + 8, 128), jnp.float32),
        in_specs=[pl.BlockSpec(memory_space=pltpu.SMEM), pl.BlockSpec(memory_space=pltpu.HBM)]
        + [pl.BlockSpec(memory_space=pltpu.VMEM)] * 7,
        out_specs=pl.BlockSpec(memory_space=pltpu.VMEM),
        scratch_shapes=[
            pltpu.VMEM((R, 128), jnp.bfloat16),
            pltpu.VMEM((128, C), jnp.bfloat16),
            pltpu.VMEM((16, 2 * SH), jnp.float32),
            pltpu.SemaphoreType.DMA,
        ],
        compiler_params=pltpu.CompilerParams(vmem_limit_bytes=12 << 20),
    )(own, rows, mates, ris, cols, colid, *tcol)


def inverse_norm(p):
    return lax.rsqrt(jnp.sum(p * p, axis=1, keepdims=True) + EPS)


def prep_body(p_ref, mate_ref, pay_ref, low_ref, one, sems):
    p = p_ref[...]
    low = (p * inverse_norm(p)).astype(jnp.bfloat16)
    m = mate_ref[...].reshape(1, SH)
    m = jnp.concatenate([m[:, 0:128], jnp.concatenate([m[:, 128:], jnp.zeros((1, 64), jnp.int32)], axis=1)], axis=0)
    hi = (m >> 8).astype(jnp.float32)
    lo = (m & 255).astype(jnp.float32)
    code = jnp.concatenate([hi, lo, jnp.zeros((12, 128), jnp.float32)], axis=0).astype(jnp.bfloat16)
    one[0:SH, :] = low
    one[SH:PADR, :] = code
    copies = [pltpu.make_async_copy(one, pay_ref.at[d], sems.at[d]) for d in range(NB)]
    for copy in copies:
        copy.start()
    low_ref[...] = low
    for copy in copies:
        copy.wait()


def prep(p, mate):
    return pl.pallas_call(
        prep_body,
        out_shape=(
            jax.ShapeDtypeStruct((NB, PADR, 128), jnp.bfloat16),
            jax.ShapeDtypeStruct((SH, 128), jnp.bfloat16),
        ),
        in_specs=[pl.BlockSpec(memory_space=pltpu.VMEM)] * 2,
        out_specs=(pl.BlockSpec(memory_space=pltpu.HBM), pl.BlockSpec(memory_space=pltpu.VMEM)),
        scratch_shapes=[pltpu.VMEM((PADR, 128), jnp.bfloat16), pltpu.SemaphoreType.DMA((NB,))],
        compiler_params=pltpu.CompilerParams(vmem_limit_bytes=6 << 20),
    )(p, mate)


def final_body(p_ref, g_ref, loss_ref, grad_ref):
    p = p_ref[...]
    inv = inverse_norm(p)
    unit = p * inv
    g = g_ref[0]
    for d in range(1, NB):
        g = g + g_ref[d]
    loss_ref[0, 0] = jnp.sum(g[SH:]) / (NA * NB * SH)
    gu = g[:SH]
    inner = jnp.sum(unit * gu, axis=1, keepdims=True)
    grad_ref[...] = inv * (gu - unit * inner)


def final(p, g):
    return pl.pallas_call(
        final_body,
        out_shape=(
            jax.ShapeDtypeStruct((1, 1), jnp.float32),
            jax.ShapeDtypeStruct((SH, 128), jnp.float32),
        ),
        in_specs=[pl.BlockSpec(memory_space=pltpu.VMEM)] * 2,
        out_specs=(pl.BlockSpec(memory_space=pltpu.SMEM), pl.BlockSpec(memory_space=pltpu.VMEM)),
        compiler_params=pltpu.CompilerParams(vmem_limit_bytes=6 << 20),
    )(p, g)


def swap(value):
    return lax.ppermute(value, "c", [(0, 1), (1, 0)])


def seat(z, core):
    z = z % NZ
    return ((z % 4) * 2 + core) * 2 + z // 4


def along_z(value, k):
    pairs = []
    for z in range(NZ):
        pairs.append((seat(z, 0), seat(z + k, 0)))
        pairs.append((seat(z, 1), seat(z - k, 1)))
    return lax.ppermute(value, ZC, pairs)


def body(projections, partner):
    xy = lax.axis_index(XY)
    z = lax.axis_index(("zh", "zl"))
    core = lax.axis_index("c")
    own = jnp.stack([xy, z, core, core]).astype(jnp.int32)
    pay, low = prep(projections, partner)
    rows = lax.all_to_all(pay, XY, 0, 0)
    pair = jnp.stack([low, swap(low)])
    direct = [along_z(pair, k) for k in (1, 2, 3)] + [along_z(low, 4)]
    crossed = [swap(piece) for piece in direct]
    pieces = [pair, *direct[:3], *crossed[:3], direct[3], crossed[3]]
    p = jnp.arange(16 * CH, dtype=jnp.int32)
    zp = (z + p // (2 * SH)) % NZ
    shard = (zp % 4) * 4 + (p // SH % 2) * 2 + zp // 4
    colid = ((xy * NA + shard) * SH + p % SH).astype(jnp.float32).reshape(16, CH)
    trow, tcol, cols, rows, mates = k1(own, rows, pieces, colid)
    trow = lax.all_to_all(trow, XY, 0, 0)
    chip = tcol + swap(tcol)
    far = [along_z(chip, k) for k in (1, 2, 3)]
    far.append(lax.ppermute(chip, ZC, [(seat(z, 0), seat(z + 4, 0)) for z in range(NZ)]))
    ris, part = mid(trow, far)
    g = k2(own, rows, mates, ris, cols, colid, (chip, part, swap(part)))
    g = lax.all_to_all(g, XY, 0, 0)
    loss, grad = final(projections, g)
    return (loss[0, 0], grad)


def solution(mesh):
    finer = Mesh(mesh.devices.reshape(4, 4, 4, 2, mesh.shape["sub"]), AXES)
    in_specs = (P(AXES, None), P(AXES))
    out_specs = (P(), P(AXES, None))
    return jax.shard_map(body, mesh=finer, in_specs=in_specs, out_specs=out_specs, check_vma=False)
```

```python
import jax
import jax.numpy as jnp
from jax import lax
from jax.experimental import pallas as pl
from jax.experimental.pallas import tpu as pltpu
from jax.sharding import Mesh
from jax.sharding import PartitionSpec as P

AXES = ("x", "y", "zl", "c", "zh")
XY = ("x", "y")
ZC = ("zl", "c", "zh")
EPS = 1e-06
NZ = 8
LOG2E = 1.4426950408889634
TAU = 0.1
KS = LOG2E / TAU
SH = 192
PADR = 208
NB = 16
NA = 16
C = NA * SH
R = NB * SH
CH = 256
T1 = 1536
N1 = R // T1
PER1 = T1 // SH
T2 = 768
N2 = R // T2
PER2 = T2 // SH
NCH = C // CH
SUB = 64
CW = 256
NW = C // CW


def col_bcast(row):
    return jnp.transpose(jnp.broadcast_to(row, (128, row.shape[1])))


def load_rows(rows_ref, rows, mates, s):
    rows[pl.ds(s * SH, SH), :] = rows_ref[s, 0:SH, :]
    code = rows_ref[s, SH:PADR, :]
    code = code.astype(jnp.float32)
    m = code[0:2] * 256.0 + code[2:4]
    mates[pl.ds(s * SH, 128), :] = col_bcast(m[0:1])
    mates[pl.ds(s * SH + 128, 64), :] = col_bcast(m[1:2])[: SH - 128]


def diag_rows(b, count):
    r = lax.broadcasted_iota(jnp.int32, (count, 128), 0) - (b % (count // SH)) * SH
    return jnp.where((r >= 0) & (r < SH), r, -100000)


def diag_of(rid, lane_at, core):
    lanes = lax.broadcasted_iota(jnp.int32, (1, 128), 1) + (lane_at - core * SH)
    return rid == lanes


def k1_body(own_ref, rows_ref, pair_ref, d1, d2, d3, s1, s2, s3, d4, s4, colid_ref,
            keep_ref, give_ref, cols_ref, rows_out, mates, rows, colsT, racc, hval, cacc, tr, tc, tail, sems):
    b = own_ref[0]
    z = own_ref[1]
    core = own_ref[2]

    places = [(pair_ref.at[0], core), (pair_ref.at[1], 1 - core), (d4, 8 + core), (s4, 9 - core)]
    for off, ref in ((-1, d1), (-2, d2), (-3, d3), (1, s1), (2, s2), (3, s3)):
        slot = jnp.where(core == 0, off & 7, (-off) & 7) * 2
        first = core if off < 0 else 1 - core
        places += [(ref.at[0], slot + first), (ref.at[1], slot + 1 - first)]
    copies = []
    for n, (piece, slot) in enumerate(places):
        to = cols_ref.at[pl.ds(pl.multiple_of(slot * SH, SH), SH), :]
        copies.append(pltpu.make_async_copy(piece, to, sems.at[n]))
    for copy in copies:
        copy.start()
    for q in range(NB):
        load_rows(rows_ref, rows, mates, q)
    for copy in copies:
        copy.wait()
    keep = pltpu.make_async_copy(rows, rows_out, sems.at[16])
    keep.start()
    for c in range(NCH):
        colsT[:, c * CH : (c + 1) * CH] = jnp.transpose(cols_ref[c * CH : (c + 1) * CH, :])
    cacc[...] = jnp.zeros_like(cacc)

    def tile(t, masked):
        at = pl.multiple_of(t * T1, T1)
        u = rows[pl.ds(at, T1), :]
        rid = diag_rows(b, T1) if masked else None
        for c in range(NW):
            s = jnp.dot(u, colsT[:, c * CW : (c + 1) * CW], preferred_element_type=jnp.float32)
            sums = [None] * (CW // 128)
            for r in range(0, T1, SUB):
                m = mates[pl.ds(pl.multiple_of(at + r, SUB), SUB), :]
                ra = None if c == 0 else racc[r : r + SUB, :]
                hv = jnp.zeros((SUB, 128), jnp.float32) if c == 0 else hval[r : r + SUB, :]
                for l in range(0, CW, 128):
                    p = c * CW + l
                    sl = s[r : r + SUB, l : l + 128]
                    el = jnp.exp2(sl * KS)
                    if masked and p < 2 * SH:
                        el = jnp.where(diag_of(rid[r : r + SUB], p, core), 0.0, el)
                    ra = el if ra is None else ra + el
                    hv = jnp.where(m == colid_ref[p // 256 : p // 256 + 1, p % 256 : p % 256 + 128], sl, hv)
                    cs = jnp.sum(el.reshape(SUB // 8, 8, 128), axis=0)
                    sums[l // 128] = cs if r == 0 else sums[l // 128] + cs
                racc[r : r + SUB, :] = ra
                hval[r : r + SUB, :] = hv
            for l in range(0, CW, 128):
                cacc[:, c * CW + l : c * CW + l + 128] += sums[l // 128]
        for q in range(PER1):
            part = jnp.sum(jnp.transpose(racc[q * SH : (q + 1) * SH, :]), axis=0, keepdims=True)
            tr[pl.ds(t * PER1 + q, 1), 0:SH] = part
        return jnp.sum(hval[...].reshape(T1 // 8, 8, 128), axis=0)

    tr[...] = jnp.ones_like(tr)
    own_tile = b // PER1
    pos = tile(own_tile, True)

    def step(k, pos):
        return pos + tile((own_tile + k) & (N1 - 1), False)

    pos = lax.fori_loop(1, N1, step, pos)
    total = jnp.sum(cacc[...], axis=0, keepdims=True)
    for k in range(NZ):
        at = (z + k) & 7
        tc[pl.ds(at, 1), :] = total[:, k * 2 * SH : k * 2 * SH + 256]
        tail[pl.ds(at, 1), :] = total[:, k * 2 * SH + 256 : (k + 1) * 2 * SH]
    by_rows = tr[...]
    by_cols = jnp.concatenate([tc[...], jnp.concatenate([tail[...], pos], axis=1)], axis=0)
    keep_ref[...] = jnp.where(core == 0, by_rows, by_cols)
    give_ref[...] = jnp.where(core == 0, by_cols, by_rows)
    keep.wait()


def k1(own, rows, pieces, colid):
    return pl.pallas_call(
        k1_body,
        out_shape=(
            jax.ShapeDtypeStruct((16, 256), jnp.float32),
            jax.ShapeDtypeStruct((16, 256), jnp.float32),
            jax.ShapeDtypeStruct((C, 128), jnp.bfloat16),
            pltpu.HBM((R, 128), jnp.bfloat16),
            jax.ShapeDtypeStruct((R, 128), jnp.float32),
        ),
        in_specs=[pl.BlockSpec(memory_space=pltpu.SMEM), pl.BlockSpec(memory_space=pltpu.VMEM)]
        + [pl.BlockSpec(memory_space=pltpu.HBM)] * len(pieces)
        + [pl.BlockSpec(memory_space=pltpu.VMEM)],
        out_specs=(
            pl.BlockSpec(memory_space=pltpu.VMEM),
            pl.BlockSpec(memory_space=pltpu.VMEM),
            pl.BlockSpec(memory_space=pltpu.VMEM),
            pl.BlockSpec(memory_space=pltpu.HBM),
            pl.BlockSpec(memory_space=pltpu.VMEM),
        ),
        scratch_shapes=[
            pltpu.VMEM((R, 128), jnp.bfloat16),
            pltpu.VMEM((128, C), jnp.bfloat16),
            pltpu.VMEM((T1, 128), jnp.float32),
            pltpu.VMEM((T1, 128), jnp.float32),
            pltpu.VMEM((8, C), jnp.float32),
            pltpu.VMEM((NB, 256), jnp.float32),
            pltpu.VMEM((8, 256), jnp.float32),
            pltpu.VMEM((8, 128), jnp.float32),
            pltpu.SemaphoreType.DMA((17,)),
        ],
        compiler_params=pltpu.CompilerParams(vmem_limit_bytes=12 << 20),
    )(own, rows, *pieces, colid)


def pack_body(own_ref, keep_ref, got_ref, pay_ref, both, sems):
    core = own_ref[2]
    mine = keep_ref[...]
    got = got_ref[...]
    both[0] = mine + jnp.where(core == 0, 0.0, got)
    both[1] = got
    copies = [pltpu.make_async_copy(both, pay_ref.at[d], sems.at[d]) for d in range(NB)]
    for copy in copies:
        copy.start()
    for copy in copies:
        copy.wait()


def pack(own, keep, got):
    return pl.pallas_call(
        pack_body,
        out_shape=pltpu.HBM((NB, 2, 16, 256), jnp.float32),
        in_specs=[pl.BlockSpec(memory_space=pltpu.SMEM)] + [pl.BlockSpec(memory_space=pltpu.VMEM)] * 2,
        out_specs=pl.BlockSpec(memory_space=pltpu.HBM),
        scratch_shapes=[pltpu.VMEM((2, 16, 256), jnp.float32), pltpu.SemaphoreType.DMA((NB,))],
        compiler_params=pltpu.CompilerParams(vmem_limit_bytes=6 << 20),
    )(own, keep, got)


def mid_body(own_ref, part_ref, keep_ref, give_ref):
    core = own_ref[2]
    line = own_ref[3]

    def total(lo, hi, which):
        out = part_ref[lo, which]
        for d in range(lo + 1, hi):
            out = out + part_ref[d, which]
        return out

    low = total(0, 8, 0)
    high = total(8, 16, 0)
    rows = low + high
    other = total(0, 16, 1)
    cols = jnp.where(line == 0, low, high)
    keep_ref[...] = jnp.where(core == 0, rows, cols)
    give_ref[...] = jnp.where(core == 0, other, cols)


def mid(own, part):
    return pl.pallas_call(
        mid_body,
        out_shape=(jax.ShapeDtypeStruct((16, 256), jnp.float32),) * 2,
        in_specs=[pl.BlockSpec(memory_space=pltpu.SMEM), pl.BlockSpec(memory_space=pltpu.VMEM)],
        out_specs=(pl.BlockSpec(memory_space=pltpu.VMEM),) * 2,
        compiler_params=pltpu.CompilerParams(vmem_limit_bytes=6 << 20),
    )(own, part)


def k2_body(own_ref, rows_in, mates, cols_ref, colid_ref, keep_ref, got_ref, g_ref, rows, ris, colsT, rcol, sem):
    fetch = pltpu.make_async_copy(rows_in, rows, sem)
    fetch.start()
    b = own_ref[0]
    z = own_ref[1]
    core = own_ref[2]
    for c in range(NCH):
        colsT[:, c * CH : (c + 1) * CH] = jnp.transpose(cols_ref[c * CH : (c + 1) * CH, :])
    mine = keep_ref[...]
    got = got_ref[...]
    by_rows = jnp.where(core == 0, mine, got)
    by_cols = jnp.where(core == 0, got, mine)
    rrow = (1.0 / TAU) / by_rows
    for q in range(NB):
        ris[q * SH : (q + 1) * SH, :] = col_bcast(rrow[q : q + 1, 0:SH])
    tall = jnp.concatenate([by_cols[0:8], by_cols[8:16, 0:128]], axis=1)
    logs = jnp.sum(jnp.log(tall), axis=0, keepdims=True)
    pos = jnp.sum(by_cols[8:16, 128:256], axis=0, keepdims=True)
    loss = logs[:, 0:128] + logs[:, 128:256] + logs[:, 256:384] - pos * (1.0 / TAU)
    loss = jnp.concatenate([loss, jnp.zeros((7, 128), jnp.float32)], axis=0)
    for d in range(NB):
        g_ref[d, SH : SH + 8, :] = loss
    rcol[8:16, :] = (1.0 / TAU) / tall
    for k in range(NZ):
        rcol[k : k + 1, :] = rcol[pl.ds(8 + ((z + k) & 7), 1), :]

    def tile(t, masked):
        at = pl.multiple_of(t * T2, T2)
        u = rows[pl.ds(at, T2), :]
        rid = diag_rows(b, T2) if masked else None
        acc = jnp.zeros((T2, 128), jnp.float32)
        for c in range(NW):
            s = jnp.dot(u, colsT[:, c * CW : (c + 1) * CW], preferred_element_type=jnp.float32)
            blocks = []
            for r in range(0, T2, SUB):
                here = pl.ds(pl.multiple_of(at + r, SUB), SUB)
                m = mates[here, :]
                ri = ris[here, :]
                ws = []
                for l in range(0, CW, 128):
                    p = c * CW + l
                    rj = rcol[p // 384 : p // 384 + 1, p % 384 : p % 384 + 128]
                    w = jnp.exp2(s[r : r + SUB, l : l + 128] * KS) * (ri + rj)
                    w = jnp.where(m == colid_ref[p // 256 : p // 256 + 1, p % 256 : p % 256 + 128], w - 2.0 / TAU, w)
                    if masked and p < 2 * SH:
                        w = jnp.where(diag_of(rid[r : r + SUB], p, core), 0.0, w)
                    ws.append(w.astype(jnp.bfloat16))
                blocks.append(jnp.concatenate(ws, axis=1))
            w = jnp.concatenate(blocks, axis=0)
            acc = acc + jnp.dot(w, cols_ref[c * CW : (c + 1) * CW, :], preferred_element_type=jnp.float32)
        for q in range(PER2):
            g_ref[t * PER2 + q, 0:SH, :] = acc[q * SH : (q + 1) * SH]

    fetch.wait()
    own_tile = b // PER2
    tile(own_tile, True)

    def step(k, _):
        tile((own_tile + k) & (N2 - 1), False)
        return 0

    lax.fori_loop(1, N2, step, 0)


def k2(own, rows, mates, cols, colid, keep, got):
    return pl.pallas_call(
        k2_body,
        out_shape=jax.ShapeDtypeStruct((NB, SH + 8, 128), jnp.float32),
        in_specs=[pl.BlockSpec(memory_space=pltpu.SMEM), pl.BlockSpec(memory_space=pltpu.HBM)]
        + [pl.BlockSpec(memory_space=pltpu.VMEM)] * 5,
        out_specs=pl.BlockSpec(memory_space=pltpu.VMEM),
        scratch_shapes=[
            pltpu.VMEM((R, 128), jnp.bfloat16),
            pltpu.VMEM((R, 128), jnp.float32),
            pltpu.VMEM((128, C), jnp.bfloat16),
            pltpu.VMEM((16, 2 * SH), jnp.float32),
            pltpu.SemaphoreType.DMA,
        ],
        compiler_params=pltpu.CompilerParams(vmem_limit_bytes=12 << 20),
    )(own, rows, mates, cols, colid, keep, got)


def inverse_norm(p):
    return lax.rsqrt(jnp.sum(p * p, axis=1, keepdims=True) + EPS)


def prep_body(p_ref, mate_ref, pay_ref, low_ref, one, sems):
    p = p_ref[...]
    low = (p * inverse_norm(p)).astype(jnp.bfloat16)
    m = mate_ref[...].reshape(1, SH)
    m = jnp.concatenate([m[:, 0:128], jnp.concatenate([m[:, 128:], jnp.zeros((1, 64), jnp.int32)], axis=1)], axis=0)
    hi = (m >> 8).astype(jnp.float32)
    lo = (m & 255).astype(jnp.float32)
    code = jnp.concatenate([hi, lo, jnp.zeros((12, 128), jnp.float32)], axis=0).astype(jnp.bfloat16)
    one[0:SH, :] = low
    one[SH:PADR, :] = code
    copies = [pltpu.make_async_copy(one, pay_ref.at[d], sems.at[d]) for d in range(NB)]
    for copy in copies:
        copy.start()
    low_ref[...] = low
    for copy in copies:
        copy.wait()


def prep(p, mate):
    return pl.pallas_call(
        prep_body,
        out_shape=(
            pltpu.HBM((NB, PADR, 128), jnp.bfloat16),
            jax.ShapeDtypeStruct((SH, 128), jnp.bfloat16),
        ),
        in_specs=[pl.BlockSpec(memory_space=pltpu.VMEM)] * 2,
        out_specs=(pl.BlockSpec(memory_space=pltpu.HBM), pl.BlockSpec(memory_space=pltpu.VMEM)),
        scratch_shapes=[pltpu.VMEM((PADR, 128), jnp.bfloat16), pltpu.SemaphoreType.DMA((NB,))],
        compiler_params=pltpu.CompilerParams(vmem_limit_bytes=6 << 20),
    )(p, mate)


def final_body(p_ref, g_ref, loss_ref, grad_ref):
    p = p_ref[...]
    inv = inverse_norm(p)
    unit = p * inv
    g = g_ref[0]
    for d in range(1, NB):
        g = g + g_ref[d]
    loss_ref[0, 0] = jnp.sum(g[SH:]) / (NA * NB * SH)
    gu = g[:SH]
    inner = jnp.sum(unit * gu, axis=1, keepdims=True)
    grad_ref[...] = inv * (gu - unit * inner)


def final(p, g):
    return pl.pallas_call(
        final_body,
        out_shape=(
            jax.ShapeDtypeStruct((1, 1), jnp.float32),
            jax.ShapeDtypeStruct((SH, 128), jnp.float32),
        ),
        in_specs=[pl.BlockSpec(memory_space=pltpu.VMEM)] * 2,
        out_specs=(pl.BlockSpec(memory_space=pltpu.SMEM), pl.BlockSpec(memory_space=pltpu.VMEM)),
        compiler_params=pltpu.CompilerParams(vmem_limit_bytes=6 << 20),
    )(p, g)


def swap(value):
    return lax.ppermute(value, "c", [(0, 1), (1, 0)])


def seat(z, core):
    z = z % NZ
    return ((z % 4) * 2 + core) * 2 + z // 4


def total_groups():
    def place(x, y, z, core):
        return ((x * 4 + y) * 4 + z % 4) * 4 + core * 2 + z // 4

    planes = [[place(x, y, z, 0) for x in range(4) for y in range(4)] for z in range(NZ)]
    lines = [[place(x, 2 * h + y, z, 1) for y in (0, 1) for z in range(NZ)] for x in range(4) for h in (0, 1)]
    return planes + lines


def along_z(value, k):
    pairs = []
    for z in range(NZ):
        pairs.append((seat(z, 0), seat(z + k, 0)))
        pairs.append((seat(z, 1), seat(z - k, 1)))
    return lax.ppermute(value, ZC, pairs)


def body(projections, partner):
    xy = lax.axis_index(XY)
    z = lax.axis_index(("zh", "zl"))
    core = lax.axis_index("c")
    own = jnp.stack([xy, z, core, lax.axis_index("y") % 2]).astype(jnp.int32)
    pay, low = prep(projections, partner)
    rows = lax.all_to_all(pay, XY, 0, 0)
    pair = jnp.stack([low, swap(low)])
    direct = [along_z(pair, k) for k in (1, 2, 3)] + [along_z(low, 4)]
    crossed = [swap(piece) for piece in direct]
    pieces = [pair, *direct[:3], *crossed[:3], direct[3], crossed[3]]
    p = jnp.arange(16 * CH, dtype=jnp.int32)
    zp = (z + p // (2 * SH)) % NZ
    shard = (zp % 4) * 4 + (p // SH % 2) * 2 + zp // 4
    colid = ((xy * NA + shard) * SH + p % SH).astype(jnp.float32).reshape(16, CH)
    pieces = [pltpu.with_memory_space_constraint(piece, pltpu.HBM) for piece in pieces]
    keep, give, cols, rows, mates = k1(own, rows, pieces, colid)
    part = lax.all_to_all(pack(own, keep, swap(give)), AXES, 0, 0, axis_index_groups=total_groups())
    keep, give = mid(own, part)
    rows = pltpu.with_memory_space_constraint(rows, pltpu.HBM)
    g = k2(own, rows, mates, cols, colid, keep, swap(give))
    g = pltpu.with_memory_space_constraint(lax.all_to_all(g, XY, 0, 0), pltpu.HBM)
    loss, grad = final(projections, g)
    return (loss[0, 0], grad)


def solution(mesh):
    finer = Mesh(mesh.devices.reshape(4, 4, 4, 2, mesh.shape["sub"]), AXES)
    in_specs = (P(AXES, None), P(AXES))
    out_specs = (P(), P(AXES, None))
    return jax.shard_map(body, mesh=finer, in_specs=in_specs, out_specs=out_specs, check_vma=False)
```

```python
import jax
import jax.numpy as jnp
from jax import lax
from jax.experimental import pallas as pl
from jax.experimental.pallas import tpu as pltpu
from jax.sharding import Mesh
from jax.sharding import PartitionSpec as P

AXES = ("x", "y", "zl", "c", "zh")
XY = ("x", "y")
ZC = ("zl", "c", "zh")
EPS = 1e-06
NZ = 8
LOG2E = 1.4426950408889634
TAU = 0.1
KS = LOG2E / TAU
SH = 192
PADR = 208
NB = 16
NA = 16
C = NA * SH
R = NB * SH
CH = 256
T1 = 1536
N1 = R // T1
PER1 = T1 // SH
T2 = 768
N2 = R // T2
PER2 = T2 // SH
NCH = C // CH
SUB = 64
CW = 256
NW = C // CW


def col_bcast(row):
    return jnp.transpose(jnp.broadcast_to(row, (128, row.shape[1])))


def load_rows(rows_ref, rows, mates, s):
    at = pl.multiple_of(s * SH, SH)
    rows[pl.ds(at, SH), :] = rows_ref[s, 0:SH, :]
    code = rows_ref[s, SH:PADR, :].astype(jnp.float32)
    m = code[0:2] * 256.0 + code[2:4]
    mates[pl.ds(at, 128), :] = col_bcast(m[0:1])
    mates[pl.ds(pl.multiple_of(at + 128, 64), 64), :] = col_bcast(m[1:2])[: SH - 128]


def diag_rows(b, count):
    r = lax.broadcasted_iota(jnp.int32, (count, 128), 0) - (b % (count // SH)) * SH
    return jnp.where((r >= 0) & (r < SH), r, -100000)


def diag_of(rid, lane_at, core):
    lanes = lax.broadcasted_iota(jnp.int32, (1, 128), 1) + (lane_at - core * SH)
    return rid == lanes


def kcols_body(own_ref, pair_ref, d1, d2, d3, s1, s2, s3, d4, s4, cols_ref, colsT, sems):
    core = own_ref[2]
    places = [(pair_ref.at[0], core), (pair_ref.at[1], 1 - core), (d4, 8 + core), (s4, 9 - core)]
    for off, ref in ((-1, d1), (-2, d2), (-3, d3), (1, s1), (2, s2), (3, s3)):
        slot = jnp.where(core == 0, off & 7, (-off) & 7) * 2
        first = core if off < 0 else 1 - core
        places += [(ref.at[0], slot + first), (ref.at[1], slot + 1 - first)]
    copies = []
    for n, (piece, slot) in enumerate(places):
        to = cols_ref.at[pl.ds(pl.multiple_of(slot * SH, SH), SH), :]
        copies.append(pltpu.make_async_copy(piece, to, sems.at[n]))
    for copy in copies:
        copy.start()
    for copy in copies:
        copy.wait()
    for c in range(NCH):
        colsT[:, c * CH : (c + 1) * CH] = jnp.transpose(cols_ref[c * CH : (c + 1) * CH, :])


def kcols(own, pieces):
    return pl.pallas_call(
        kcols_body,
        out_shape=(
            jax.ShapeDtypeStruct((C, 128), jnp.bfloat16),
            jax.ShapeDtypeStruct((128, C), jnp.bfloat16),
        ),
        in_specs=[pl.BlockSpec(memory_space=pltpu.SMEM)] + [pl.BlockSpec(memory_space=pltpu.HBM)] * len(pieces),
        out_specs=(pl.BlockSpec(memory_space=pltpu.VMEM),) * 2,
        scratch_shapes=[pltpu.SemaphoreType.DMA((16,))],
        compiler_params=pltpu.CompilerParams(vmem_limit_bytes=6 << 20),
        cost_estimate=pl.CostEstimate(flops=8*10**9, transcendentals=0, bytes_accessed=1 << 21),
    )(own, *pieces)


def k1_body(own_ref, rows_ref, colsT, colid_ref, keep_ref, give_ref, rows_out, mates, rows, racc, hval, cacc, tr, tc, sems):
    b = own_ref[0]
    z = own_ref[1]
    core = own_ref[2]
    cacc[...] = jnp.zeros_like(cacc)

    def tile(t, masked):
        at = pl.multiple_of(t * T1, T1)
        for q in range(PER1):
            load_rows(rows_ref, rows, mates, t * PER1 + q)
        u = rows[pl.ds(at, T1), :]
        rid = diag_rows(b, T1) if masked else None
        for c in range(NW):
            s = jnp.dot(u, colsT[:, c * CW : (c + 1) * CW], preferred_element_type=jnp.float32)
            sums = [None] * (CW // 128)
            for r in range(0, T1, SUB):
                m = mates[pl.ds(pl.multiple_of(at + r, SUB), SUB), :]
                ra = None if c == 0 else racc[r : r + SUB, :]
                hv = jnp.zeros((SUB, 128), jnp.float32) if c == 0 else hval[r : r + SUB, :]
                for l in range(0, CW, 128):
                    p = c * CW + l
                    sl = s[r : r + SUB, l : l + 128]
                    el = jnp.exp2(sl * KS)
                    if masked and p < 2 * SH:
                        el = jnp.where(diag_of(rid[r : r + SUB], p, core), 0.0, el)
                    ra = el if ra is None else ra + el
                    hv = jnp.where(m == colid_ref[p // 256 : p // 256 + 1, p % 256 : p % 256 + 128], sl, hv)
                    cs = jnp.sum(el.reshape(SUB // 8, 8, 128), axis=0)
                    sums[l // 128] = cs if r == 0 else sums[l // 128] + cs
                racc[r : r + SUB, :] = ra
                hval[r : r + SUB, :] = hv
            for l in range(0, CW, 128):
                cacc[:, c * CW + l : c * CW + l + 128] += sums[l // 128]
        for q in range(0, PER1, 2):
            part = [jnp.sum(jnp.transpose(racc[k * SH : (k + 1) * SH, :]), axis=0, keepdims=True) for k in (q, q + 1)]
            tr[pl.ds(t * (PER1 // 2) + q // 2, 1), :] = jnp.concatenate(part, axis=1)
        return jnp.sum(hval[...].reshape(T1 // 8, 8, 128), axis=0)

    own_tile = b // PER1
    pos = tile(own_tile, True)

    def step(k, pos):
        return pos + tile((own_tile + k) & (N1 - 1), False)

    pos = lax.fori_loop(1, N1, step, pos)
    keep = pltpu.make_async_copy(rows, rows_out, sems)
    keep.start()
    total = jnp.sum(cacc[...], axis=0, keepdims=True)
    for k in range(NZ):
        tc[pl.ds((z + k) & 7, 1), :] = total[:, k * 2 * SH : (k + 1) * 2 * SH]
    none = jnp.zeros((8, 256), jnp.float32)
    by_rows = jnp.concatenate([tr[...], jnp.zeros((8, 2 * SH), jnp.float32)], axis=0)
    by_cols = jnp.concatenate([tc[...], jnp.concatenate([pos, none], axis=1)], axis=0)
    keep_ref[...] = jnp.where(core == 0, by_rows, by_cols)
    give_ref[...] = jnp.where(core == 0, by_cols, by_rows)
    keep.wait()


def k1(own, rows, colsT, colid):
    return pl.pallas_call(
        k1_body,
        out_shape=(
            jax.ShapeDtypeStruct((16, 2 * SH), jnp.float32),
            jax.ShapeDtypeStruct((16, 2 * SH), jnp.float32),
            pltpu.HBM((R, 128), jnp.bfloat16),
            jax.ShapeDtypeStruct((R, 128), jnp.float32),
        ),
        in_specs=[pl.BlockSpec(memory_space=pltpu.SMEM)] + [pl.BlockSpec(memory_space=pltpu.VMEM)] * 3,
        out_specs=(
            pl.BlockSpec(memory_space=pltpu.VMEM),
            pl.BlockSpec(memory_space=pltpu.VMEM),
            pl.BlockSpec(memory_space=pltpu.HBM),
            pl.BlockSpec(memory_space=pltpu.VMEM),
        ),
        scratch_shapes=[
            pltpu.VMEM((R, 128), jnp.bfloat16),
            pltpu.VMEM((T1, 128), jnp.float32),
            pltpu.VMEM((T1, 128), jnp.float32),
            pltpu.VMEM((8, C), jnp.float32),
            pltpu.VMEM((8, 2 * SH), jnp.float32),
            pltpu.VMEM((8, 2 * SH), jnp.float32),
            pltpu.SemaphoreType.DMA,
        ],
        compiler_params=pltpu.CompilerParams(vmem_limit_bytes=12 << 20),
    )(own, rows, colsT, colid)


def pack_body(own_ref, keep_ref, got_ref, pay_ref, both, sems):
    core = own_ref[2]
    mine = keep_ref[...]
    got = got_ref[...]
    low = jnp.where(core == 0, mine[0:8], mine[0:8] + got[0:8])
    high = jnp.where(core == 0, got[0:8], mine[8:16] + got[8:16])
    both[...] = jnp.concatenate([low, high], axis=0)
    copies = [pltpu.make_async_copy(both, pay_ref.at[d], sems.at[d]) for d in range(NB)]
    for copy in copies:
        copy.start()
    for copy in copies:
        copy.wait()


def pack(own, keep, got):
    return pl.pallas_call(
        pack_body,
        out_shape=pltpu.HBM((NB, 16, 2 * SH), jnp.float32),
        in_specs=[pl.BlockSpec(memory_space=pltpu.SMEM)] + [pl.BlockSpec(memory_space=pltpu.VMEM)] * 2,
        out_specs=pl.BlockSpec(memory_space=pltpu.HBM),
        scratch_shapes=[pltpu.VMEM((16, 2 * SH), jnp.float32), pltpu.SemaphoreType.DMA((NB,))],
        compiler_params=pltpu.CompilerParams(vmem_limit_bytes=6 << 20),
    )(own, keep, got)


def mid_body(own_ref, part_ref, keep_ref, give_ref):
    core = own_ref[2]
    line = own_ref[3]

    def total(lo, hi):
        out = part_ref[lo]
        for d in range(lo + 1, hi):
            out = out + part_ref[d]
        return out

    low = total(0, 8)
    high = total(8, 16)
    rows = low + high
    cols = jnp.where(line == 0, low, high)
    keep_ref[...] = jnp.where(core == 0, rows, cols)
    give_ref[...] = jnp.where(core == 0, jnp.concatenate([rows[8:16], rows[0:8]], axis=0), cols)


def mid(own, part):
    return pl.pallas_call(
        mid_body,
        out_shape=(jax.ShapeDtypeStruct((16, 2 * SH), jnp.float32),) * 2,
        in_specs=[pl.BlockSpec(memory_space=pltpu.SMEM), pl.BlockSpec(memory_space=pltpu.VMEM)],
        out_specs=(pl.BlockSpec(memory_space=pltpu.VMEM),) * 2,
        compiler_params=pltpu.CompilerParams(vmem_limit_bytes=6 << 20),
    )(own, part)


def k2_body(own_ref, rows_in, mates, cols_ref, colsT, colid_ref, keep_ref, got_ref, g_ref, rows, ris, rrow, rcol, sem):
    fetch = pltpu.make_async_copy(rows_in, rows, sem)
    fetch.start()
    b = own_ref[0]
    z = own_ref[1]
    core = own_ref[2]
    mine = keep_ref[...]
    got = got_ref[...]
    by_rows = jnp.where(core == 0, mine, got)
    by_cols = jnp.where(core == 0, got, mine)
    rrow[...] = (1.0 / TAU) / by_rows[0:8]
    tall = by_cols[0:8]
    logs = jnp.sum(jnp.log(tall), axis=0, keepdims=True)
    pos = jnp.sum(by_cols[8:16, 0:128], axis=0, keepdims=True)
    loss = logs[:, 0:128] + logs[:, 128:256] + logs[:, 256:384] - pos * (1.0 / TAU)
    loss = jnp.concatenate([loss, jnp.zeros((7, 128), jnp.float32)], axis=0)
    for d in range(NB):
        g_ref[d, SH : SH + 8, :] = loss
    rcol[8:16, :] = (1.0 / TAU) / tall
    for k in range(NZ):
        rcol[k : k + 1, :] = rcol[pl.ds(8 + ((z + k) & 7), 1), :]

    def tile(t, masked):
        at = pl.multiple_of(t * T2, T2)
        for q in range(0, PER2, 2):
            two = rrow[pl.ds(t * (PER2 // 2) + q // 2, 1), :]
            ris[q * SH : (q + 2) * SH, :] = col_bcast(two)
        u = rows[pl.ds(at, T2), :]
        rid = diag_rows(b, T2) if masked else None
        acc = jnp.zeros((T2, 128), jnp.float32)
        for c in range(NW):
            s = jnp.dot(u, colsT[:, c * CW : (c + 1) * CW], preferred_element_type=jnp.float32)
            blocks = []
            for r in range(0, T2, SUB):
                here = pl.ds(pl.multiple_of(at + r, SUB), SUB)
                m = mates[here, :]
                ri = ris[r : r + SUB, :]
                ws = []
                for l in range(0, CW, 128):
                    p = c * CW + l
                    rj = rcol[p // 384 : p // 384 + 1, p % 384 : p % 384 + 128]
                    w = jnp.exp2(s[r : r + SUB, l : l + 128] * KS) * (ri + rj)
                    w = jnp.where(m == colid_ref[p // 256 : p // 256 + 1, p % 256 : p % 256 + 128], w - 2.0 / TAU, w)
                    if masked and p < 2 * SH:
                        w = jnp.where(diag_of(rid[r : r + SUB], p, core), 0.0, w)
                    ws.append(w.astype(jnp.bfloat16))
                blocks.append(jnp.concatenate(ws, axis=1))
            w = jnp.concatenate(blocks, axis=0)
            acc = acc + jnp.dot(w, cols_ref[c * CW : (c + 1) * CW, :], preferred_element_type=jnp.float32)
        for q in range(PER2):
            g_ref[t * PER2 + q, 0:SH, :] = acc[q * SH : (q + 1) * SH]

    fetch.wait()
    own_tile = b // PER2
    tile(own_tile, True)

    def step(k, _):
        tile((own_tile + k) & (N2 - 1), False)
        return 0

    lax.fori_loop(1, N2, step, 0)


def k2(own, rows, mates, cols, colsT, colid, keep, got):
    return pl.pallas_call(
        k2_body,
        out_shape=jax.ShapeDtypeStruct((NB, SH + 8, 128), jnp.float32),
        in_specs=[pl.BlockSpec(memory_space=pltpu.SMEM), pl.BlockSpec(memory_space=pltpu.HBM)]
        + [pl.BlockSpec(memory_space=pltpu.VMEM)] * 6,
        out_specs=pl.BlockSpec(memory_space=pltpu.VMEM),
        scratch_shapes=[
            pltpu.VMEM((R, 128), jnp.bfloat16),
            pltpu.VMEM((T2, 128), jnp.float32),
            pltpu.VMEM((8, 2 * SH), jnp.float32),
            pltpu.VMEM((16, 2 * SH), jnp.float32),
            pltpu.SemaphoreType.DMA,
        ],
        compiler_params=pltpu.CompilerParams(vmem_limit_bytes=12 << 20),
    )(own, rows, mates, cols, colsT, colid, keep, got)


def inverse_norm(p):
    return lax.rsqrt(jnp.sum(p * p, axis=1, keepdims=True) + EPS)


def prep_body(p_hbm, mate_hbm, q_ref, pay_ref, pair_ref, low_ref, p_ref, mate_ref, one, sems):
    first = pltpu.make_async_copy(p_hbm, p_ref, sems.at[NB])
    second = pltpu.make_async_copy(mate_hbm, mate_ref, sems.at[NB + 1])
    first.start()
    second.start()
    q = q_ref[...]
    pair_ref[1] = (q * inverse_norm(q)).astype(jnp.bfloat16)
    first.wait()
    second.wait()
    p = p_ref[...]
    low = (p * inverse_norm(p)).astype(jnp.bfloat16)
    m = mate_ref[...].reshape(1, SH)
    m = jnp.concatenate([m[:, 0:128], jnp.concatenate([m[:, 128:], jnp.zeros((1, 64), jnp.int32)], axis=1)], axis=0)
    hi = (m >> 8).astype(jnp.float32)
    lo = (m & 255).astype(jnp.float32)
    code = jnp.concatenate([hi, lo, jnp.zeros((12, 128), jnp.float32)], axis=0).astype(jnp.bfloat16)
    one[0:SH, :] = low
    one[SH:PADR, :] = code
    copies = [pltpu.make_async_copy(one, pay_ref.at[d], sems.at[d]) for d in range(NB)]
    for copy in copies:
        copy.start()
    pair_ref[0] = low
    low_ref[...] = low
    for copy in copies:
        copy.wait()


def prep(p, mate, q):
    return pl.pallas_call(
        prep_body,
        out_shape=(
            pltpu.HBM((NB, PADR, 128), jnp.bfloat16),
            jax.ShapeDtypeStruct((2, SH, 128), jnp.bfloat16),
            jax.ShapeDtypeStruct((SH, 128), jnp.bfloat16),
        ),
        in_specs=[pl.BlockSpec(memory_space=pltpu.HBM)] * 2 + [pl.BlockSpec(memory_space=pltpu.VMEM)],
        out_specs=(pl.BlockSpec(memory_space=pltpu.HBM),) + (pl.BlockSpec(memory_space=pltpu.VMEM),) * 2,
        scratch_shapes=[
            pltpu.VMEM((SH, 128), jnp.float32),
            pltpu.VMEM((SH,), jnp.int32),
            pltpu.VMEM((PADR, 128), jnp.bfloat16),
            pltpu.SemaphoreType.DMA((NB + 2,)),
        ],
        compiler_params=pltpu.CompilerParams(vmem_limit_bytes=6 << 20),
    )(p, mate, q)


def final_body(p_ref, g_ref, loss_ref, grad_ref):
    p = p_ref[...]
    inv = inverse_norm(p)
    unit = p * inv
    g = g_ref[0]
    for d in range(1, NB):
        g = g + g_ref[d]
    loss_ref[0, 0] = jnp.sum(g[SH:]) / (NA * NB * SH)
    gu = g[:SH]
    inner = jnp.sum(unit * gu, axis=1, keepdims=True)
    grad_ref[...] = inv * (gu - unit * inner)


def final(p, g):
    return pl.pallas_call(
        final_body,
        out_shape=(
            jax.ShapeDtypeStruct((1, 1), jnp.float32),
            jax.ShapeDtypeStruct((SH, 128), jnp.float32),
        ),
        in_specs=[pl.BlockSpec(memory_space=pltpu.VMEM)] * 2,
        out_specs=(pl.BlockSpec(memory_space=pltpu.SMEM), pl.BlockSpec(memory_space=pltpu.VMEM)),
        compiler_params=pltpu.CompilerParams(vmem_limit_bytes=6 << 20),
    )(p, g)


def swap(value):
    return lax.ppermute(value, "c", [(0, 1), (1, 0)])


def seat(z, core):
    z = z % NZ
    return ((z % 4) * 2 + core) * 2 + z // 4


def total_groups():
    def place(x, y, z, core):
        return ((x * 4 + y) * 4 + z % 4) * 4 + core * 2 + z // 4

    planes = [[place(x, y, z, 0) for x in range(4) for y in range(4)] for z in range(NZ)]
    lines = [[place(x, 2 * h + y, z, 1) for y in (0, 1) for z in range(NZ)] for x in range(4) for h in (0, 1)]
    return planes + lines


def along_z(value, k):
    pairs = []
    for z in range(NZ):
        pairs.append((seat(z, 0), seat(z + k, 0)))
        pairs.append((seat(z, 1), seat(z - k, 1)))
    return lax.ppermute(value, ZC, pairs)


def body(projections, partner):
    xy = lax.axis_index(XY)
    z = lax.axis_index(("zh", "zl"))
    core = lax.axis_index("c")
    own = jnp.stack([xy, z, core, lax.axis_index("y") % 2]).astype(jnp.int32)
    near = pltpu.with_memory_space_constraint(projections, pltpu.HBM)
    mate = pltpu.with_memory_space_constraint(partner, pltpu.HBM)
    pay, pair, low = prep(near, mate, swap(projections))
    rows = lax.all_to_all(pay, XY, 0, 0)
    direct = [along_z(pair, k) for k in (1, 2, 3)] + [along_z(low, 4)]
    crossed = [swap(piece) for piece in direct]
    pieces = [pair, *direct[:3], *crossed[:3], direct[3], crossed[3]]
    p = jnp.arange(16 * CH, dtype=jnp.int32)
    zp = (z + p // (2 * SH)) % NZ
    shard = (zp % 4) * 4 + (p // SH % 2) * 2 + zp // 4
    colid = ((xy * NA + shard) * SH + p % SH).astype(jnp.float32).reshape(16, CH)
    pieces = [pltpu.with_memory_space_constraint(piece, pltpu.HBM) for piece in pieces]
    cols, colsT = kcols(own, pieces)
    keep, give, rows, mates = k1(own, rows, colsT, colid)
    part = lax.all_to_all(pack(own, keep, swap(give)), AXES, 0, 0, axis_index_groups=total_groups())
    keep, give = mid(own, part)
    rows = pltpu.with_memory_space_constraint(rows, pltpu.HBM)
    g = k2(own, rows, mates, cols, colsT, colid, keep, swap(give))
    g = lax.all_to_all(g, XY, 0, 0)
    loss, grad = final(projections, g)
    return (loss[0, 0], grad)


def solution(mesh):
    finer = Mesh(mesh.devices.reshape(4, 4, 4, 2, mesh.shape["sub"]), AXES)
    in_specs = (P(AXES, None), P(AXES))
    out_specs = (P(), P(AXES, None))
    return jax.shard_map(body, mesh=finer, in_specs=in_specs, out_specs=out_specs, check_vma=False)
```

```python
import jax
import jax.numpy as jnp
from jax import lax
from jax.experimental import pallas as pl
from jax.experimental.pallas import tpu as pltpu
from jax.sharding import Mesh
from jax.sharding import PartitionSpec as P

AXES = ("x", "y", "zl", "c", "zh")
XY = ("x", "y")
ZC = ("zl", "c", "zh")
EPS = 1e-06
NZ = 8
LOG2E = 1.4426950408889634
TAU = 0.1
KS = LOG2E / TAU
SH = 192
PADR = 208
NB = 16
NA = 16
C = NA * SH
R = NB * SH
CH = 256
T1 = 1536
N1 = R // T1
PER1 = T1 // SH
T2 = 768
N2 = R // T2
PER2 = T2 // SH
NCH = C // CH
SUB = 64
CW = 256
NW = C // CW


def col_bcast(row):
    return jnp.transpose(jnp.broadcast_to(row, (128, row.shape[1])))


def load_rows(rows_ref, rows, mates, s):
    at = pl.multiple_of(s * SH, SH)
    rows[pl.ds(at, SH), :] = rows_ref[s, 0:SH, :]
    code = rows_ref[s, SH:PADR, :].astype(jnp.float32)
    m = code[0:2] * 256.0 + code[2:4]
    mates[pl.ds(at, 128), :] = col_bcast(m[0:1])
    mates[pl.ds(pl.multiple_of(at + 128, 64), 64), :] = col_bcast(m[1:2])[: SH - 128]


def diag_rows(b, count):
    r = lax.broadcasted_iota(jnp.int32, (count, 128), 0) - (b % (count // SH)) * SH
    return jnp.where((r >= 0) & (r < SH), r, -100000)


def diag_of(rid, lane_at, core):
    lanes = lax.broadcasted_iota(jnp.int32, (1, 128), 1) + (lane_at - core * SH)
    return rid == lanes


def kcols_body(own_ref, pair_ref, d1, d2, d3, s1, s2, s3, d4, s4, cols_ref, colsT, sems):
    core = own_ref[2]
    places = [(pair_ref.at[0], core), (pair_ref.at[1], 1 - core), (d4, 8 + core), (s4, 9 - core)]
    for off, ref in ((-1, d1), (-2, d2), (-3, d3), (1, s1), (2, s2), (3, s3)):
        slot = jnp.where(core == 0, off & 7, (-off) & 7) * 2
        first = core if off < 0 else 1 - core
        places += [(ref.at[0], slot + first), (ref.at[1], slot + 1 - first)]
    copies = []
    for n, (piece, slot) in enumerate(places):
        to = cols_ref.at[pl.ds(pl.multiple_of(slot * SH, SH), SH), :]
        copies.append(pltpu.make_async_copy(piece, to, sems.at[n]))
    for copy in copies:
        copy.start()
    for copy in copies:
        copy.wait()
    for c in range(NCH):
        colsT[:, c * CH : (c + 1) * CH] = jnp.transpose(cols_ref[c * CH : (c + 1) * CH, :])


def kcols(own, pieces):
    return pl.pallas_call(
        kcols_body,
        out_shape=(
            jax.ShapeDtypeStruct((C, 128), jnp.bfloat16),
            jax.ShapeDtypeStruct((128, C), jnp.bfloat16),
        ),
        in_specs=[pl.BlockSpec(memory_space=pltpu.SMEM)] + [pl.BlockSpec(memory_space=pltpu.HBM)] * len(pieces),
        out_specs=(pl.BlockSpec(memory_space=pltpu.VMEM),) * 2,
        scratch_shapes=[pltpu.SemaphoreType.DMA((16,))],
        compiler_params=pltpu.CompilerParams(vmem_limit_bytes=6 << 20),
        cost_estimate=pl.CostEstimate(flops=10**9, transcendentals=0, bytes_accessed=1 << 21),
    )(own, *pieces)


def k1_body(own_ref, rows_ref, colsT, colid_ref, keep_ref, give_ref, rows_out, mates, rows, racc, hval, cacc, tr, tc, sems):
    b = own_ref[0]
    z = own_ref[1]
    core = own_ref[2]
    cacc[...] = jnp.zeros_like(cacc)

    def tile(t, masked):
        at = pl.multiple_of(t * T1, T1)
        for q in range(PER1):
            load_rows(rows_ref, rows, mates, t * PER1 + q)
        u = rows[pl.ds(at, T1), :]
        rid = diag_rows(b, T1) if masked else None
        for c in range(NW):
            s = jnp.dot(u, colsT[:, c * CW : (c + 1) * CW], preferred_element_type=jnp.float32)
            sums = [None] * (CW // 128)
            for r in range(0, T1, SUB):
                m = mates[pl.ds(pl.multiple_of(at + r, SUB), SUB), :]
                ra = None if c == 0 else racc[r : r + SUB, :]
                hv = jnp.zeros((SUB, 128), jnp.float32) if c == 0 else hval[r : r + SUB, :]
                for l in range(0, CW, 128):
                    p = c * CW + l
                    sl = s[r : r + SUB, l : l + 128]
                    el = jnp.exp2(sl * KS)
                    if masked and p < 2 * SH:
                        el = jnp.where(diag_of(rid[r : r + SUB], p, core), 0.0, el)
                    ra = el if ra is None else ra + el
                    hv = jnp.where(m == colid_ref[p // 256 : p // 256 + 1, p % 256 : p % 256 + 128], sl, hv)
                    cs = jnp.sum(el.reshape(SUB // 8, 8, 128), axis=0)
                    sums[l // 128] = cs if r == 0 else sums[l // 128] + cs
                racc[r : r + SUB, :] = ra
                hval[r : r + SUB, :] = hv
            for l in range(0, CW, 128):
                cacc[:, c * CW + l : c * CW + l + 128] += sums[l // 128]
        for q in range(0, PER1, 2):
            part = [jnp.sum(jnp.transpose(racc[k * SH : (k + 1) * SH, :]), axis=0, keepdims=True) for k in (q, q + 1)]
            tr[pl.ds(t * (PER1 // 2) + q // 2, 1), :] = jnp.concatenate(part, axis=1)
        return jnp.sum(hval[...].reshape(T1 // 8, 8, 128), axis=0)

    own_tile = b // PER1
    pos = tile(own_tile, True)

    def step(k, pos):
        return pos + tile((own_tile + k) & (N1 - 1), False)

    pos = lax.fori_loop(1, N1, step, pos)
    keep = pltpu.make_async_copy(rows, rows_out, sems)
    keep.start()
    total = jnp.sum(cacc[...], axis=0, keepdims=True)
    for k in range(NZ):
        tc[pl.ds((z + k) & 7, 1), :] = total[:, k * 2 * SH : (k + 1) * 2 * SH]
    none = jnp.zeros((8, 256), jnp.float32)
    by_rows = jnp.concatenate([tr[...], jnp.zeros((8, 2 * SH), jnp.float32)], axis=0)
    by_cols = jnp.concatenate([tc[...], jnp.concatenate([pos, none], axis=1)], axis=0)
    keep_ref[...] = jnp.where(core == 0, by_rows, by_cols)
    give_ref[...] = jnp.where(core == 0, by_cols, by_rows)
    keep.wait()


def k1(own, rows, colsT, colid):
    return pl.pallas_call(
        k1_body,
        out_shape=(
            jax.ShapeDtypeStruct((16, 2 * SH), jnp.float32),
            jax.ShapeDtypeStruct((16, 2 * SH), jnp.float32),
            pltpu.HBM((R, 128), jnp.bfloat16),
            jax.ShapeDtypeStruct((R, 128), jnp.float32),
        ),
        in_specs=[pl.BlockSpec(memory_space=pltpu.SMEM)] + [pl.BlockSpec(memory_space=pltpu.VMEM)] * 3,
        out_specs=(
            pl.BlockSpec(memory_space=pltpu.VMEM),
            pl.BlockSpec(memory_space=pltpu.VMEM),
            pl.BlockSpec(memory_space=pltpu.HBM),
            pl.BlockSpec(memory_space=pltpu.VMEM),
        ),
        scratch_shapes=[
            pltpu.VMEM((R, 128), jnp.bfloat16),
            pltpu.VMEM((T1, 128), jnp.float32),
            pltpu.VMEM((T1, 128), jnp.float32),
            pltpu.VMEM((8, C), jnp.float32),
            pltpu.VMEM((8, 2 * SH), jnp.float32),
            pltpu.VMEM((8, 2 * SH), jnp.float32),
            pltpu.SemaphoreType.DMA,
        ],
        compiler_params=pltpu.CompilerParams(vmem_limit_bytes=12 << 20),
    )(own, rows, colsT, colid)


def pack_body(own_ref, keep_ref, got_ref, pay_ref, both, sems):
    core = own_ref[2]
    mine = keep_ref[...]
    got = got_ref[...]
    low = jnp.where(core == 0, mine[0:8], mine[0:8] + got[0:8])
    high = jnp.where(core == 0, got[0:8], mine[8:16] + got[8:16])
    both[...] = jnp.concatenate([low, high], axis=0)
    copies = [pltpu.make_async_copy(both, pay_ref.at[d], sems.at[d]) for d in range(NB)]
    for copy in copies:
        copy.start()
    for copy in copies:
        copy.wait()


def pack(own, keep, got):
    return pl.pallas_call(
        pack_body,
        out_shape=pltpu.HBM((NB, 16, 2 * SH), jnp.float32),
        in_specs=[pl.BlockSpec(memory_space=pltpu.SMEM)] + [pl.BlockSpec(memory_space=pltpu.VMEM)] * 2,
        out_specs=pl.BlockSpec(memory_space=pltpu.HBM),
        scratch_shapes=[pltpu.VMEM((16, 2 * SH), jnp.float32), pltpu.SemaphoreType.DMA((NB,))],
        compiler_params=pltpu.CompilerParams(vmem_limit_bytes=6 << 20),
    )(own, keep, got)


def mid_body(own_ref, part_ref, keep_ref, give_ref):
    core = own_ref[2]
    line = own_ref[3]

    def total(lo, hi):
        out = part_ref[lo]
        for d in range(lo + 1, hi):
            out = out + part_ref[d]
        return out

    low = total(0, 8)
    high = total(8, 16)
    rows = low + high
    cols = jnp.where(line == 0, low, high)
    keep_ref[...] = jnp.where(core == 0, rows, cols)
    give_ref[...] = jnp.where(core == 0, jnp.concatenate([rows[8:16], rows[0:8]], axis=0), cols)


def mid(own, part):
    return pl.pallas_call(
        mid_body,
        out_shape=(jax.ShapeDtypeStruct((16, 2 * SH), jnp.float32),) * 2,
        in_specs=[pl.BlockSpec(memory_space=pltpu.SMEM), pl.BlockSpec(memory_space=pltpu.VMEM)],
        out_specs=(pl.BlockSpec(memory_space=pltpu.VMEM),) * 2,
        compiler_params=pltpu.CompilerParams(vmem_limit_bytes=6 << 20),
    )(own, part)


def k2_body(own_ref, rows_in, mates, cols_ref, colsT, colid_ref, keep_ref, got_ref, g_ref, rows, ris, rrow, rcol, sem):
    fetch = pltpu.make_async_copy(rows_in, rows, sem)
    fetch.start()
    b = own_ref[0]
    z = own_ref[1]
    core = own_ref[2]
    mine = keep_ref[...]
    got = got_ref[...]
    by_rows = jnp.where(core == 0, mine, got)
    by_cols = jnp.where(core == 0, got, mine)
    rrow[...] = (1.0 / TAU) / by_rows[0:8]
    tall = by_cols[0:8]
    logs = jnp.sum(jnp.log(tall), axis=0, keepdims=True)
    pos = jnp.sum(by_cols[8:16, 0:128], axis=0, keepdims=True)
    loss = logs[:, 0:128] + logs[:, 128:256] + logs[:, 256:384] - pos * (1.0 / TAU)
    loss = jnp.concatenate([loss, jnp.zeros((7, 128), jnp.float32)], axis=0)
    for d in range(NB):
        g_ref[d, SH : SH + 8, :] = loss
    rcol[8:16, :] = (1.0 / TAU) / tall
    for k in range(NZ):
        rcol[k : k + 1, :] = rcol[pl.ds(8 + ((z + k) & 7), 1), :]

    def tile(t, masked):
        at = pl.multiple_of(t * T2, T2)
        for q in range(0, PER2, 2):
            two = rrow[pl.ds(t * (PER2 // 2) + q // 2, 1), :]
            ris[q * SH : (q + 2) * SH, :] = col_bcast(two)
        u = rows[pl.ds(at, T2), :]
        rid = diag_rows(b, T2) if masked else None
        acc = jnp.zeros((T2, 128), jnp.float32)
        for c in range(NW):
            s = jnp.dot(u, colsT[:, c * CW : (c + 1) * CW], preferred_element_type=jnp.float32)
            blocks = []
            for r in range(0, T2, SUB):
                here = pl.ds(pl.multiple_of(at + r, SUB), SUB)
                m = mates[here, :]
                ri = ris[r : r + SUB, :]
                ws = []
                for l in range(0, CW, 128):
                    p = c * CW + l
                    rj = rcol[p // 384 : p // 384 + 1, p % 384 : p % 384 + 128]
                    w = jnp.exp2(s[r : r + SUB, l : l + 128] * KS) * (ri + rj)
                    w = jnp.where(m == colid_ref[p // 256 : p // 256 + 1, p % 256 : p % 256 + 128], w - 2.0 / TAU, w)
                    if masked and p < 2 * SH:
                        w = jnp.where(diag_of(rid[r : r + SUB], p, core), 0.0, w)
                    ws.append(w.astype(jnp.bfloat16))
                blocks.append(jnp.concatenate(ws, axis=1))
            w = jnp.concatenate(blocks, axis=0)
            acc = acc + jnp.dot(w, cols_ref[c * CW : (c + 1) * CW, :], preferred_element_type=jnp.float32)
        for q in range(PER2):
            g_ref[t * PER2 + q, 0:SH, :] = acc[q * SH : (q + 1) * SH]

    fetch.wait()
    own_tile = b // PER2
    tile(own_tile, True)

    def step(k, _):
        tile((own_tile + k) & (N2 - 1), False)
        return 0

    lax.fori_loop(1, N2, step, 0)


def k2(own, rows, mates, cols, colsT, colid, keep, got):
    return pl.pallas_call(
        k2_body,
        out_shape=jax.ShapeDtypeStruct((NB, SH + 8, 128), jnp.float32),
        in_specs=[pl.BlockSpec(memory_space=pltpu.SMEM), pl.BlockSpec(memory_space=pltpu.HBM)]
        + [pl.BlockSpec(memory_space=pltpu.VMEM)] * 6,
        out_specs=pl.BlockSpec(memory_space=pltpu.VMEM),
        scratch_shapes=[
            pltpu.VMEM((R, 128), jnp.bfloat16),
            pltpu.VMEM((T2, 128), jnp.float32),
            pltpu.VMEM((8, 2 * SH), jnp.float32),
            pltpu.VMEM((16, 2 * SH), jnp.float32),
            pltpu.SemaphoreType.DMA,
        ],
        compiler_params=pltpu.CompilerParams(vmem_limit_bytes=12 << 20),
    )(own, rows, mates, cols, colsT, colid, keep, got)


def inverse_norm(p):
    return lax.rsqrt(jnp.sum(p * p, axis=1, keepdims=True) + EPS)


def prep_body(p_hbm, mate_hbm, pay_ref, low_ref, p_ref, mate_ref, one, sems):
    first = pltpu.make_async_copy(p_hbm, p_ref, sems.at[NB])
    second = pltpu.make_async_copy(mate_hbm, mate_ref, sems.at[NB + 1])
    first.start()
    second.start()
    first.wait()
    second.wait()
    p = p_ref[...]
    low = (p * inverse_norm(p)).astype(jnp.bfloat16)
    m = mate_ref[...].reshape(1, SH)
    m = jnp.concatenate([m[:, 0:128], jnp.concatenate([m[:, 128:], jnp.zeros((1, 64), jnp.int32)], axis=1)], axis=0)
    hi = (m >> 8).astype(jnp.float32)
    lo = (m & 255).astype(jnp.float32)
    code = jnp.concatenate([hi, lo, jnp.zeros((12, 128), jnp.float32)], axis=0).astype(jnp.bfloat16)
    one[0:SH, :] = low
    one[SH:PADR, :] = code
    copies = [pltpu.make_async_copy(one, pay_ref.at[d], sems.at[d]) for d in range(NB)]
    for copy in copies:
        copy.start()
    low_ref[...] = low
    for copy in copies:
        copy.wait()


def prep(p, mate):
    return pl.pallas_call(
        prep_body,
        out_shape=(
            pltpu.HBM((NB, PADR, 128), jnp.bfloat16),
            jax.ShapeDtypeStruct((SH, 128), jnp.bfloat16),
        ),
        in_specs=[pl.BlockSpec(memory_space=pltpu.HBM)] * 2,
        out_specs=(pl.BlockSpec(memory_space=pltpu.HBM), pl.BlockSpec(memory_space=pltpu.VMEM)),
        scratch_shapes=[
            pltpu.VMEM((SH, 128), jnp.float32),
            pltpu.VMEM((SH,), jnp.int32),
            pltpu.VMEM((PADR, 128), jnp.bfloat16),
            pltpu.SemaphoreType.DMA((NB + 2,)),
        ],
        compiler_params=pltpu.CompilerParams(vmem_limit_bytes=6 << 20),
    )(p, mate)


def final_body(p_ref, g_ref, loss_ref, grad_ref):
    p = p_ref[...]
    inv = inverse_norm(p)
    unit = p * inv
    g = g_ref[0]
    for d in range(1, NB):
        g = g + g_ref[d]
    loss_ref[0, 0] = jnp.sum(g[SH:]) / (NA * NB * SH)
    gu = g[:SH]
    inner = jnp.sum(unit * gu, axis=1, keepdims=True)
    grad_ref[...] = inv * (gu - unit * inner)


def final(p, g):
    return pl.pallas_call(
        final_body,
        out_shape=(
            jax.ShapeDtypeStruct((1, 1), jnp.float32),
            jax.ShapeDtypeStruct((SH, 128), jnp.float32),
        ),
        in_specs=[pl.BlockSpec(memory_space=pltpu.VMEM)] * 2,
        out_specs=(pl.BlockSpec(memory_space=pltpu.SMEM), pl.BlockSpec(memory_space=pltpu.VMEM)),
        compiler_params=pltpu.CompilerParams(vmem_limit_bytes=6 << 20),
    )(p, g)


def swap(value):
    return lax.ppermute(value, "c", [(0, 1), (1, 0)])


def seat(z, core):
    z = z % NZ
    return ((z % 4) * 2 + core) * 2 + z // 4


def total_groups():
    def place(x, y, z, core):
        return ((x * 4 + y) * 4 + z % 4) * 4 + core * 2 + z // 4

    planes = [[place(x, y, z, 0) for x in range(4) for y in range(4)] for z in range(NZ)]
    lines = [[place(x, 2 * h + y, z, 1) for y in (0, 1) for z in range(NZ)] for x in range(4) for h in (0, 1)]
    return planes + lines


def along_z(value, k):
    pairs = []
    for z in range(NZ):
        pairs.append((seat(z, 0), seat(z + k, 0)))
        pairs.append((seat(z, 1), seat(z - k, 1)))
    return lax.ppermute(value, ZC, pairs)


def body(projections, partner):
    xy = lax.axis_index(XY)
    z = lax.axis_index(("zh", "zl"))
    core = lax.axis_index("c")
    own = jnp.stack([xy, z, core, lax.axis_index("y") % 2]).astype(jnp.int32)
    pay, low = prep(pltpu.with_memory_space_constraint(projections, pltpu.HBM), pltpu.with_memory_space_constraint(partner, pltpu.HBM))
    rows = lax.all_to_all(pay, XY, 0, 0)
    pair = jnp.stack([low, swap(low)])
    direct = [along_z(pair, k) for k in (1, 2, 3)] + [along_z(low, 4)]
    crossed = [swap(piece) for piece in direct]
    pieces = [pair, *direct[:3], *crossed[:3], direct[3], crossed[3]]
    p = jnp.arange(16 * CH, dtype=jnp.int32)
    zp = (z + p // (2 * SH)) % NZ
    shard = (zp % 4) * 4 + (p // SH % 2) * 2 + zp // 4
    colid = ((xy * NA + shard) * SH + p % SH).astype(jnp.float32).reshape(16, CH)
    pieces = [pltpu.with_memory_space_constraint(piece, pltpu.HBM) for piece in pieces]
    cols, colsT = kcols(own, pieces)
    keep, give, rows, mates = k1(own, rows, colsT, colid)
    part = lax.all_to_all(pack(own, keep, swap(give)), AXES, 0, 0, axis_index_groups=total_groups())
    keep, give = mid(own, part)
    rows = pltpu.with_memory_space_constraint(rows, pltpu.HBM)
    g = k2(own, rows, mates, cols, colsT, colid, keep, swap(give))
    g = lax.all_to_all(g, XY, 0, 0)
    loss, grad = final(projections, g)
    return (loss[0, 0], grad)


def solution(mesh):
    finer = Mesh(mesh.devices.reshape(4, 4, 4, 2, mesh.shape["sub"]), AXES)
    in_specs = (P(AXES, None), P(AXES))
    out_specs = (P(), P(AXES, None))
    return jax.shard_map(body, mesh=finer, in_specs=in_specs, out_specs=out_specs, check_vma=False)
```

```python
import jax
import jax.numpy as jnp
from jax import lax
from jax.experimental import pallas as pl
from jax.experimental.pallas import tpu as pltpu
from jax.sharding import Mesh
from jax.sharding import PartitionSpec as P

AXES = ("x", "y", "zl", "c", "zh")
XY = ("x", "y")
ZC = ("zl", "c", "zh")
EPS = 1e-06
NZ = 8
LOG2E = 1.4426950408889634
TAU = 0.1
KS = LOG2E / TAU
SH = 192
PADR = 208
NB = 16
NA = 16
C = NA * SH
R = NB * SH
CH = 256
T1 = 1536
N1 = R // T1
PER1 = T1 // SH
T2 = 768
N2 = R // T2
PER2 = T2 // SH
NCH = C // CH
SUB = 64
CW = 256
NW = C // CW


def col_bcast(row):
    return jnp.transpose(jnp.broadcast_to(row, (128, row.shape[1])))


def load_rows(rows_ref, rows, mates, s):
    at = pl.multiple_of(s * SH, SH)
    rows[pl.ds(at, SH), :] = rows_ref[s, 0:SH, :]
    code = rows_ref[s, SH:PADR, :].astype(jnp.float32)
    m = code[0:2] * 256.0 + code[2:4]
    mates[pl.ds(at, 128), :] = col_bcast(m[0:1])
    mates[pl.ds(pl.multiple_of(at + 128, 64), 64), :] = col_bcast(m[1:2])[: SH - 128]


def diag_rows(b, count):
    r = lax.broadcasted_iota(jnp.int32, (count, 128), 0) - (b % (count // SH)) * SH
    return jnp.where((r >= 0) & (r < SH), r, -100000)


def diag_of(rid, lane_at, core):
    lanes = lax.broadcasted_iota(jnp.int32, (1, 128), 1) + (lane_at - core * SH)
    return rid == lanes


def chip_at(k, z, core):
    far = (k + 1) // 2
    return (z + jnp.where(core == 0, 1, -1) * (-far if k % 2 else far)) & (NZ - 1)


def place_columns(places, cols_ref, colsT, sems):
    copies = []
    for n, (piece, slot) in enumerate(places):
        to = cols_ref.at[pl.ds(pl.multiple_of(slot * SH, SH), SH), :]
        copies.append(pltpu.make_async_copy(piece, to, sems.at[n]))
    for copy in copies:
        copy.start()
    for copy in copies:
        copy.wait()
    for c in range(NCH // 2):
        colsT[:, c * CH : (c + 1) * CH] = jnp.transpose(cols_ref[c * CH : (c + 1) * CH, :])


def early_body(own_ref, pair_ref, d1, s1, d2, cols_ref, colsT, sems):
    core = own_ref[2]
    places = []
    for slot, ref, first in ((0, pair_ref, core), (2, d1, core), (4, s1, 1 - core), (6, d2, core)):
        places += [(ref.at[0], slot + first), (ref.at[1], slot + 1 - first)]
    place_columns(places, cols_ref, colsT, sems)


def late_body(own_ref, s2, d3, s3, d4, s4, after, cols_ref, colsT, sems):
    core = own_ref[2]
    places = [(d4, 6 + core), (s4, 7 - core)]
    for slot, ref, first in ((0, s2, 1 - core), (2, d3, core), (4, s3, 1 - core)):
        places += [(ref.at[0], slot + first), (ref.at[1], slot + 1 - first)]
    place_columns(places, cols_ref, colsT, sems)


def kcols(place, own, pieces, flops):
    return pl.pallas_call(
        place,
        out_shape=(
            jax.ShapeDtypeStruct((C // 2, 128), jnp.bfloat16),
            jax.ShapeDtypeStruct((128, C // 2), jnp.bfloat16),
        ),
        in_specs=[pl.BlockSpec(memory_space=pltpu.SMEM)] + [pl.BlockSpec(memory_space=pltpu.HBM)] * len(pieces),
        out_specs=(pl.BlockSpec(memory_space=pltpu.VMEM),) * 2,
        scratch_shapes=[pltpu.SemaphoreType.DMA((8,))],
        compiler_params=pltpu.CompilerParams(vmem_limit_bytes=6 << 20),
        cost_estimate=pl.CostEstimate(flops=flops, transcendentals=0, bytes_accessed=1 << 20),
    )(own, *pieces)


def score_tile(at, base, b, core, rows, mates, colsT, colid_ref, racc, hval, cacc):
    u = rows[pl.ds(at, T1), :]
    rid = None if b is None else diag_rows(b, T1)
    for c in range(NW // 2):
        s = jnp.dot(u, colsT[:, c * CW : (c + 1) * CW], preferred_element_type=jnp.float32)
        sums = [None] * (CW // 128)
        for r in range(0, T1, SUB):
            m = mates[pl.ds(pl.multiple_of(at + r, SUB), SUB), :]
            ra = None if c == 0 else racc[r : r + SUB, :]
            hv = jnp.zeros((SUB, 128), jnp.float32) if c == 0 else hval[r : r + SUB, :]
            for l in range(0, CW, 128):
                p = c * CW + l
                sl = s[r : r + SUB, l : l + 128]
                el = jnp.exp2(sl * KS)
                if rid is not None and p < 2 * SH:
                    el = jnp.where(diag_of(rid[r : r + SUB], p, core), 0.0, el)
                ra = el if ra is None else ra + el
                hv = jnp.where(m == colid_ref[base + p // 256 : base + p // 256 + 1, p % 256 : p % 256 + 128], sl, hv)
                cs = jnp.sum(el.reshape(SUB // 8, 8, 128), axis=0)
                sums[l // 128] = cs if r == 0 else sums[l // 128] + cs
            racc[r : r + SUB, :] = ra
            hval[r : r + SUB, :] = hv
        for l in range(0, CW, 128):
            cacc[:, c * CW + l : c * CW + l + 128] += sums[l // 128]
    parts = []
    for q in range(0, PER1, 2):
        part = [jnp.sum(jnp.transpose(racc[k * SH : (k + 1) * SH, :]), axis=0, keepdims=True) for k in (q, q + 1)]
        parts.append(jnp.concatenate(part, axis=1))
    return parts, jnp.sum(hval[...].reshape(T1 // 8, 8, 128), axis=0)


def k1a_body(own_ref, rows_ref, colsT, colid_ref, tr, tc, pos_ref, rows_out, mates, rows, racc, hval, cacc, sem):
    b = own_ref[0]
    z = own_ref[1]
    core = own_ref[2]
    cacc[...] = jnp.zeros_like(cacc)
    tc[...] = jnp.zeros_like(tc)

    def tile(t, own_b):
        at = pl.multiple_of(t * T1, T1)
        for q in range(PER1):
            load_rows(rows_ref, rows, mates, t * PER1 + q)
        parts, pos = score_tile(at, 0, own_b, core, rows, mates, colsT, colid_ref, racc, hval, cacc)
        for q, part in enumerate(parts):
            tr[pl.ds(t * (PER1 // 2) + q, 1), :] = part
        return pos

    own_tile = b // PER1
    pos = tile(own_tile, b)
    pos_ref[...] = lax.fori_loop(1, N1, lambda k, v: v + tile((own_tile + k) & (N1 - 1), None), pos)
    keep = pltpu.make_async_copy(rows, rows_out, sem)
    keep.start()
    total = jnp.sum(cacc[...], axis=0, keepdims=True)
    for k in range(NZ // 2):
        tc[pl.ds(chip_at(k, z, core), 1), :] = total[:, k * 2 * SH : (k + 1) * 2 * SH]
    keep.wait()


def k1a(own, rows, colsT, colid):
    vmem = pl.BlockSpec(memory_space=pltpu.VMEM)
    return pl.pallas_call(
        k1a_body,
        out_shape=(
            jax.ShapeDtypeStruct((8, 2 * SH), jnp.float32),
            jax.ShapeDtypeStruct((8, 2 * SH), jnp.float32),
            jax.ShapeDtypeStruct((8, 128), jnp.float32),
            pltpu.HBM((R, 128), jnp.bfloat16),
            jax.ShapeDtypeStruct((R, 128), jnp.float32),
        ),
        in_specs=[pl.BlockSpec(memory_space=pltpu.SMEM)] + [vmem] * 3,
        out_specs=(vmem, vmem, vmem, pl.BlockSpec(memory_space=pltpu.HBM), vmem),
        scratch_shapes=[
            pltpu.VMEM((R, 128), jnp.bfloat16),
            pltpu.VMEM((T1, 128), jnp.float32),
            pltpu.VMEM((T1, 128), jnp.float32),
            pltpu.VMEM((8, C // 2), jnp.float32),
            pltpu.SemaphoreType.DMA,
        ],
        compiler_params=pltpu.CompilerParams(vmem_limit_bytes=14 << 20),
    )(own, rows, colsT, colid)


def k1b_body(own_ref, rows_ref, mates, colsT, colid_ref, tra, tca, posa, keep_ref, give_ref, rows, racc, hval, cacc, tr, tc):
    z = own_ref[1]
    core = own_ref[2]
    cacc[...] = jnp.zeros_like(cacc)
    tc[...] = tca[...]

    def tile(t, pos):
        at = pl.multiple_of(t * T1, T1)
        for q in range(PER1):
            rows[pl.ds(pl.multiple_of(at + q * SH, SH), SH), :] = rows_ref[t * PER1 + q, 0:SH, :]
        parts, more = score_tile(at, NCH // 2, None, core, rows, mates, colsT, colid_ref, racc, hval, cacc)
        for q, part in enumerate(parts):
            tr[pl.ds(t * (PER1 // 2) + q, 1), :] = part
        return pos + more

    pos = lax.fori_loop(0, N1, tile, posa[...])
    total = jnp.sum(cacc[...], axis=0, keepdims=True)
    for k in range(NZ // 2):
        tc[pl.ds(chip_at(k + NZ // 2, z, core), 1), :] = total[:, k * 2 * SH : (k + 1) * 2 * SH]
    none = jnp.zeros((8, 256), jnp.float32)
    by_rows = jnp.concatenate([tra[...] + tr[...], jnp.zeros((8, 2 * SH), jnp.float32)], axis=0)
    by_cols = jnp.concatenate([tc[...], jnp.concatenate([pos, none], axis=1)], axis=0)
    keep_ref[...] = jnp.where(core == 0, by_rows, by_cols)
    give_ref[...] = jnp.where(core == 0, by_cols, by_rows)


def k1b(own, rows, mates, colsT, colid, sums):
    vmem = pl.BlockSpec(memory_space=pltpu.VMEM)
    return pl.pallas_call(
        k1b_body,
        out_shape=(jax.ShapeDtypeStruct((16, 2 * SH), jnp.float32),) * 2,
        in_specs=[pl.BlockSpec(memory_space=pltpu.SMEM)] + [vmem] * 7,
        out_specs=(vmem, vmem),
        scratch_shapes=[
            pltpu.VMEM((R, 128), jnp.bfloat16),
            pltpu.VMEM((T1, 128), jnp.float32),
            pltpu.VMEM((T1, 128), jnp.float32),
            pltpu.VMEM((8, C // 2), jnp.float32),
            pltpu.VMEM((8, 2 * SH), jnp.float32),
            pltpu.VMEM((8, 2 * SH), jnp.float32),
        ],
        compiler_params=pltpu.CompilerParams(vmem_limit_bytes=14 << 20),
    )(own, rows, mates, colsT, colid, *sums)


def pack_body(own_ref, keep_ref, got_ref, pay_ref):
    core = own_ref[2]
    mine = keep_ref[...]
    got = got_ref[...]
    low = jnp.where(core == 0, mine[0:8], mine[0:8] + got[0:8])
    high = jnp.where(core == 0, got[0:8], mine[8:16] + got[8:16])
    both = jnp.concatenate([low, high], axis=0)
    for d in range(NB):
        pay_ref[d] = both


def pack(own, keep, got):
    return pl.pallas_call(
        pack_body,
        out_shape=jax.ShapeDtypeStruct((NB, 16, 2 * SH), jnp.float32),
        in_specs=[pl.BlockSpec(memory_space=pltpu.SMEM)] + [pl.BlockSpec(memory_space=pltpu.VMEM)] * 2,
        out_specs=pl.BlockSpec(memory_space=pltpu.VMEM),
        compiler_params=pltpu.CompilerParams(vmem_limit_bytes=6 << 20),
    )(own, keep, got)


def mid_body(own_ref, part_ref, keep_ref, give_ref):
    core = own_ref[2]
    line = own_ref[3]

    def total(lo, hi):
        out = part_ref[lo]
        for d in range(lo + 1, hi):
            out = out + part_ref[d]
        return out

    low = total(0, 8)
    high = total(8, 16)
    rows = low + high
    cols = jnp.where(line == 0, low, high)
    keep_ref[...] = jnp.where(core == 0, rows, cols)
    give_ref[...] = jnp.where(core == 0, jnp.concatenate([rows[8:16], rows[0:8]], axis=0), cols)


def mid(own, part):
    return pl.pallas_call(
        mid_body,
        out_shape=(jax.ShapeDtypeStruct((16, 2 * SH), jnp.float32),) * 2,
        in_specs=[pl.BlockSpec(memory_space=pltpu.SMEM), pl.BlockSpec(memory_space=pltpu.VMEM)],
        out_specs=(pl.BlockSpec(memory_space=pltpu.VMEM),) * 2,
        compiler_params=pltpu.CompilerParams(vmem_limit_bytes=6 << 20),
    )(own, part)


def k2_body(own_ref, rows_in, mates, colsa, colsb, colsTa, colsTb, colid_ref, keep_ref, got_ref, g_ref, rows, ris, rrow, rcol, sem):
    fetch = pltpu.make_async_copy(rows_in, rows, sem)
    fetch.start()
    b = own_ref[0]
    z = own_ref[1]
    core = own_ref[2]
    mine = keep_ref[...]
    got = got_ref[...]
    by_rows = jnp.where(core == 0, mine, got)
    by_cols = jnp.where(core == 0, got, mine)
    rrow[...] = (1.0 / TAU) / by_rows[0:8]
    tall = by_cols[0:8]
    logs = jnp.sum(jnp.log(tall), axis=0, keepdims=True)
    pos = jnp.sum(by_cols[8:16, 0:128], axis=0, keepdims=True)
    loss = logs[:, 0:128] + logs[:, 128:256] + logs[:, 256:384] - pos * (1.0 / TAU)
    loss = jnp.concatenate([loss, jnp.zeros((7, 128), jnp.float32)], axis=0)
    for d in range(NB):
        g_ref[d, SH : SH + 8, :] = loss
    rcol[8:16, :] = (1.0 / TAU) / tall
    for k in range(NZ):
        rcol[k : k + 1, :] = rcol[pl.ds(8 + chip_at(k, z, core), 1), :]

    def tile(t, masked):
        at = pl.multiple_of(t * T2, T2)
        for q in range(0, PER2, 2):
            two = rrow[pl.ds(t * (PER2 // 2) + q // 2, 1), :]
            ris[q * SH : (q + 2) * SH, :] = col_bcast(two)
        u = rows[pl.ds(at, T2), :]
        rid = diag_rows(b, T2) if masked else None
        acc = jnp.zeros((T2, 128), jnp.float32)
        for c in range(NW):
            h = c % (NW // 2)
            colsT = colsTa if c < NW // 2 else colsTb
            cols = colsa if c < NW // 2 else colsb
            s = jnp.dot(u, colsT[:, h * CW : (h + 1) * CW], preferred_element_type=jnp.float32)
            blocks = []
            for r in range(0, T2, SUB):
                here = pl.ds(pl.multiple_of(at + r, SUB), SUB)
                m = mates[here, :]
                ri = ris[r : r + SUB, :]
                ws = []
                for l in range(0, CW, 128):
                    p = c * CW + l
                    rj = rcol[p // 384 : p // 384 + 1, p % 384 : p % 384 + 128]
                    w = jnp.exp2(s[r : r + SUB, l : l + 128] * KS) * (ri + rj)
                    w = jnp.where(m == colid_ref[p // 256 : p // 256 + 1, p % 256 : p % 256 + 128], w - 2.0 / TAU, w)
                    if masked and p < 2 * SH:
                        w = jnp.where(diag_of(rid[r : r + SUB], p, core), 0.0, w)
                    ws.append(w.astype(jnp.bfloat16))
                blocks.append(jnp.concatenate(ws, axis=1))
            w = jnp.concatenate(blocks, axis=0)
            acc = acc + jnp.dot(w, cols[h * CW : (h + 1) * CW, :], preferred_element_type=jnp.float32)
        for q in range(PER2):
            g_ref[t * PER2 + q, 0:SH, :] = acc[q * SH : (q + 1) * SH]

    fetch.wait()
    own_tile = b // PER2
    tile(own_tile, True)

    def step(k, _):
        tile((own_tile + k) & (N2 - 1), False)
        return 0

    lax.fori_loop(1, N2, step, 0)


def k2(own, rows, mates, cols, colid, keep, got):
    return pl.pallas_call(
        k2_body,
        out_shape=jax.ShapeDtypeStruct((NB, SH + 8, 128), jnp.float32),
        in_specs=[pl.BlockSpec(memory_space=pltpu.SMEM), pl.BlockSpec(memory_space=pltpu.HBM)]
        + [pl.BlockSpec(memory_space=pltpu.VMEM)] * 8,
        out_specs=pl.BlockSpec(memory_space=pltpu.VMEM),
        scratch_shapes=[
            pltpu.VMEM((R, 128), jnp.bfloat16),
            pltpu.VMEM((T2, 128), jnp.float32),
            pltpu.VMEM((8, 2 * SH), jnp.float32),
            pltpu.VMEM((16, 2 * SH), jnp.float32),
            pltpu.SemaphoreType.DMA,
        ],
        compiler_params=pltpu.CompilerParams(vmem_limit_bytes=12 << 20),
    )(own, rows, mates, *cols, colid, keep, got)


def inverse_norm(p):
    return lax.rsqrt(jnp.sum(p * p, axis=1, keepdims=True) + EPS)


def prep_body(p_hbm, mate_hbm, pay_ref, low_ref, p_ref, mate_ref, one, sems):
    first = pltpu.make_async_copy(p_hbm, p_ref, sems.at[NB])
    second = pltpu.make_async_copy(mate_hbm, mate_ref, sems.at[NB + 1])
    first.start()
    second.start()
    first.wait()
    second.wait()
    p = p_ref[...]
    low = (p * inverse_norm(p)).astype(jnp.bfloat16)
    m = mate_ref[...].reshape(1, SH)
    m = jnp.concatenate([m[:, 0:128], jnp.concatenate([m[:, 128:], jnp.zeros((1, 64), jnp.int32)], axis=1)], axis=0)
    hi = (m >> 8).astype(jnp.float32)
    lo = (m & 255).astype(jnp.float32)
    code = jnp.concatenate([hi, lo, jnp.zeros((12, 128), jnp.float32)], axis=0).astype(jnp.bfloat16)
    one[0:SH, :] = low
    one[SH:PADR, :] = code
    copies = [pltpu.make_async_copy(one, pay_ref.at[d], sems.at[d]) for d in range(NB)]
    for copy in copies:
        copy.start()
    low_ref[...] = low
    for copy in copies:
        copy.wait()


def prep(p, mate):
    return pl.pallas_call(
        prep_body,
        out_shape=(
            pltpu.HBM((NB, PADR, 128), jnp.bfloat16),
            jax.ShapeDtypeStruct((SH, 128), jnp.bfloat16),
        ),
        in_specs=[pl.BlockSpec(memory_space=pltpu.HBM)] * 2,
        out_specs=(pl.BlockSpec(memory_space=pltpu.HBM), pl.BlockSpec(memory_space=pltpu.VMEM)),
        scratch_shapes=[
            pltpu.VMEM((SH, 128), jnp.float32),
            pltpu.VMEM((SH,), jnp.int32),
            pltpu.VMEM((PADR, 128), jnp.bfloat16),
            pltpu.SemaphoreType.DMA((NB + 2,)),
        ],
        compiler_params=pltpu.CompilerParams(vmem_limit_bytes=6 << 20),
    )(p, mate)


def final_body(p_ref, g_ref, loss_ref, grad_ref):
    p = p_ref[...]
    inv = inverse_norm(p)
    unit = p * inv
    g = g_ref[0]
    for d in range(1, NB):
        g = g + g_ref[d]
    loss_ref[0, 0] = jnp.sum(g[SH:]) / (NA * NB * SH)
    gu = g[:SH]
    inner = jnp.sum(unit * gu, axis=1, keepdims=True)
    grad_ref[...] = inv * (gu - unit * inner)


def final(p, g):
    return pl.pallas_call(
        final_body,
        out_shape=(
            jax.ShapeDtypeStruct((1, 1), jnp.float32),
            jax.ShapeDtypeStruct((SH, 128), jnp.float32),
        ),
        in_specs=[pl.BlockSpec(memory_space=pltpu.VMEM)] * 2,
        out_specs=(pl.BlockSpec(memory_space=pltpu.SMEM), pl.BlockSpec(memory_space=pltpu.VMEM)),
        compiler_params=pltpu.CompilerParams(vmem_limit_bytes=6 << 20),
    )(p, g)


def swap(value):
    return lax.ppermute(value, "c", [(0, 1), (1, 0)])


def seat(z, core):
    z = z % NZ
    return ((z % 4) * 2 + core) * 2 + z // 4


def total_groups():
    def place(x, y, z, core):
        return ((x * 4 + y) * 4 + z % 4) * 4 + core * 2 + z // 4

    planes = [[place(x, y, z, 0) for x in range(4) for y in range(4)] for z in range(NZ)]
    lines = [[place(x, 2 * h + y, z, 1) for y in (0, 1) for z in range(NZ)] for x in range(4) for h in (0, 1)]
    return planes + lines


def along_z(value, k):
    pairs = []
    for z in range(NZ):
        pairs.append((seat(z, 0), seat(z + k, 0)))
        pairs.append((seat(z, 1), seat(z - k, 1)))
    return lax.ppermute(value, ZC, pairs)


def body(projections, partner):
    xy = lax.axis_index(XY)
    z = lax.axis_index(("zh", "zl"))
    core = lax.axis_index("c")
    own = jnp.stack([xy, z, core, lax.axis_index("y") % 2]).astype(jnp.int32)
    pay, low = prep(pltpu.with_memory_space_constraint(projections, pltpu.HBM), pltpu.with_memory_space_constraint(partner, pltpu.HBM))
    rows = lax.all_to_all(pay, XY, 0, 0)
    pair = jnp.stack([low, swap(low)])
    direct = [along_z(pair, k) for k in (1, 2, 3)] + [along_z(low, 4)]
    crossed = [swap(piece) for piece in direct[:2]]
    d1, d2 = [pltpu.with_memory_space_constraint(piece, pltpu.HBM) for piece in direct[:2]]
    s1, s2 = [pltpu.with_memory_space_constraint(piece, pltpu.HBM) for piece in crossed]
    p = jnp.arange(16 * CH, dtype=jnp.int32)
    k = p // (2 * SH)
    far = jnp.where(k % 2 == 1, -((k + 1) // 2), k // 2)
    zp = (z + jnp.where(core == 0, far, -far)) & (NZ - 1)
    shard = (zp % 4) * 4 + (p // SH % 2) * 2 + zp // 4
    colid = ((xy * NA + shard) * SH + p % SH).astype(jnp.float32).reshape(16, CH)
    colsa, colsTa = kcols(early_body, own, [pltpu.with_memory_space_constraint(pair, pltpu.HBM), d1, s1, d2], 10**9)
    *sums, kept, mates = k1a(own, rows, colsTa, colid)
    d3, d4, after = lax.optimization_barrier((direct[2], direct[3], sums[2]))
    late = [pltpu.with_memory_space_constraint(piece, pltpu.HBM) for piece in (d3, swap(d3), d4, swap(d4))]
    colsb, colsTb = kcols(late_body, own, [s2, *late, after], 10**9)
    keep, give = k1b(own, rows, mates, colsTb, colid, sums)
    rows = kept
    part = lax.all_to_all(pack(own, keep, swap(give)), AXES, 0, 0, axis_index_groups=total_groups())
    keep, give = mid(own, part)
    rows = pltpu.with_memory_space_constraint(rows, pltpu.HBM)
    g = k2(own, rows, mates, (colsa, colsb, colsTa, colsTb), colid, keep, swap(give))
    g = lax.all_to_all(g, XY, 0, 0)
    loss, grad = final(projections, g)
    return (loss[0, 0], grad)


def solution(mesh):
    finer = Mesh(mesh.devices.reshape(4, 4, 4, 2, mesh.shape["sub"]), AXES)
    in_specs = (P(AXES, None), P(AXES))
    out_specs = (P(), P(AXES, None))
    return jax.shard_map(body, mesh=finer, in_specs=in_specs, out_specs=out_specs, check_vma=False)
```

```python
import jax
import jax.numpy as jnp
from jax import lax
from jax.experimental import pallas as pl
from jax.experimental.pallas import tpu as pltpu
from jax.sharding import Mesh
from jax.sharding import PartitionSpec as P

AXES = ("x", "y", "zl", "c", "zh")
XY = ("x", "y")
ZC = ("zl", "c", "zh")
EPS = 1e-06
NZ = 8
LOG2E = 1.4426950408889634
TAU = 0.1
KS = LOG2E / TAU
SH = 192
PADR = 208
NB = 16
NA = 16
C = NA * SH
R = NB * SH
CH = 256
T1 = 1536
N1 = R // T1
PER1 = T1 // SH
T2 = 768
N2 = R // T2
PER2 = T2 // SH
NCH = C // CH
SUB = 64
CW = 256
NW = C // CW


def col_bcast(row):
    return jnp.transpose(jnp.broadcast_to(row, (128, row.shape[1])))


def load_rows(rows_ref, rows, mates, s):
    at = pl.multiple_of(s * SH, SH)
    rows[pl.ds(at, SH), :] = rows_ref[s, 0:SH, :]
    code = rows_ref[s, SH:PADR, :].astype(jnp.float32)
    m = code[0:2] * 256.0 + code[2:4]
    mates[pl.ds(at, 128), :] = col_bcast(m[0:1])
    mates[pl.ds(pl.multiple_of(at + 128, 64), 64), :] = col_bcast(m[1:2])[: SH - 128]


def diag_rows(b, count):
    r = lax.broadcasted_iota(jnp.int32, (count, 128), 0) - (b % (count // SH)) * SH
    return jnp.where((r >= 0) & (r < SH), r, -100000)


def diag_of(rid, lane_at, core):
    lanes = lax.broadcasted_iota(jnp.int32, (1, 128), 1) + (lane_at - core * SH)
    return rid == lanes


def kcols_body(own_ref, pair_ref, d1, d2, d3, s1, s2, s3, d4, s4, cols_ref, colsT, sems):
    core = own_ref[2]
    places = [(pair_ref.at[0], core), (pair_ref.at[1], 1 - core), (d4, 8 + core), (s4, 9 - core)]
    for off, ref in ((-1, d1), (-2, d2), (-3, d3), (1, s1), (2, s2), (3, s3)):
        slot = jnp.where(core == 0, off & 7, (-off) & 7) * 2
        first = core if off < 0 else 1 - core
        places += [(ref.at[0], slot + first), (ref.at[1], slot + 1 - first)]
    copies = []
    for n, (piece, slot) in enumerate(places):
        to = cols_ref.at[pl.ds(pl.multiple_of(slot * SH, SH), SH), :]
        copies.append(pltpu.make_async_copy(piece, to, sems.at[n]))
    for copy in copies:
        copy.start()
    for copy in copies:
        copy.wait()
    for c in range(NCH):
        colsT[:, c * CH : (c + 1) * CH] = jnp.transpose(cols_ref[c * CH : (c + 1) * CH, :])


def kcols(own, pieces):
    return pl.pallas_call(
        kcols_body,
        out_shape=(
            jax.ShapeDtypeStruct((C, 128), jnp.bfloat16),
            jax.ShapeDtypeStruct((128, C), jnp.bfloat16),
        ),
        in_specs=[pl.BlockSpec(memory_space=pltpu.SMEM)] + [pl.BlockSpec(memory_space=pltpu.HBM)] * len(pieces),
        out_specs=(pl.BlockSpec(memory_space=pltpu.VMEM),) * 2,
        scratch_shapes=[pltpu.SemaphoreType.DMA((16,))],
        compiler_params=pltpu.CompilerParams(vmem_limit_bytes=6 << 20),
        cost_estimate=pl.CostEstimate(flops=10**10, transcendentals=0, bytes_accessed=1 << 21),
    )(own, *pieces)


def k1_body(own_ref, rows_ref, colsT, colid_ref, keep_ref, give_ref, rows_out, mates, rows, racc, hval, cacc, tr, tc, sems):
    b = own_ref[0]
    z = own_ref[1]
    core = own_ref[2]
    cacc[...] = jnp.zeros_like(cacc)

    def tile(t, masked):
        at = pl.multiple_of(t * T1, T1)
        for q in range(PER1):
            load_rows(rows_ref, rows, mates, t * PER1 + q)
        u = rows[pl.ds(at, T1), :]
        rid = diag_rows(b, T1) if masked else None
        for c in range(NW):
            s = jnp.dot(u, colsT[:, c * CW : (c + 1) * CW], preferred_element_type=jnp.float32)
            sums = [None] * (CW // 128)
            for r in range(0, T1, SUB):
                m = mates[pl.ds(pl.multiple_of(at + r, SUB), SUB), :]
                ra = None if c == 0 else racc[r : r + SUB, :]
                hv = jnp.zeros((SUB, 128), jnp.float32) if c == 0 else hval[r : r + SUB, :]
                for l in range(0, CW, 128):
                    p = c * CW + l
                    sl = s[r : r + SUB, l : l + 128]
                    el = jnp.exp2(sl * KS)
                    if masked and p < 2 * SH:
                        el = jnp.where(diag_of(rid[r : r + SUB], p, core), 0.0, el)
                    ra = el if ra is None else ra + el
                    hv = jnp.where(m == colid_ref[p // 256 : p // 256 + 1, p % 256 : p % 256 + 128], sl, hv)
                    cs = jnp.sum(el.reshape(SUB // 8, 8, 128), axis=0)
                    sums[l // 128] = cs if r == 0 else sums[l // 128] + cs
                racc[r : r + SUB, :] = ra
                hval[r : r + SUB, :] = hv
            for l in range(0, CW, 128):
                cacc[:, c * CW + l : c * CW + l + 128] += sums[l // 128]
        for q in range(0, PER1, 2):
            part = [jnp.sum(jnp.transpose(racc[k * SH : (k + 1) * SH, :]), axis=0, keepdims=True) for k in (q, q + 1)]
            tr[pl.ds(t * (PER1 // 2) + q // 2, 1), :] = jnp.concatenate(part, axis=1)
        return jnp.sum(hval[...].reshape(T1 // 8, 8, 128), axis=0)

    own_tile = b // PER1
    pos = tile(own_tile, True)

    def step(k, pos):
        return pos + tile((own_tile + k) & (N1 - 1), False)

    pos = lax.fori_loop(1, N1, step, pos)
    keep = pltpu.make_async_copy(rows, rows_out, sems)
    keep.start()
    total = jnp.sum(cacc[...], axis=0, keepdims=True)
    for k in range(NZ):
        tc[pl.ds((z + k) & 7, 1), :] = total[:, k * 2 * SH : (k + 1) * 2 * SH]
    none = jnp.zeros((8, 256), jnp.float32)
    by_rows = jnp.concatenate([tr[...], jnp.zeros((8, 2 * SH), jnp.float32)], axis=0)
    by_cols = jnp.concatenate([tc[...], jnp.concatenate([pos, none], axis=1)], axis=0)
    keep_ref[...] = jnp.where(core == 0, by_rows, by_cols)
    give_ref[...] = jnp.where(core == 0, by_cols, by_rows)
    keep.wait()


def k1(own, rows, colsT, colid):
    return pl.pallas_call(
        k1_body,
        out_shape=(
            jax.ShapeDtypeStruct((16, 2 * SH), jnp.float32),
            jax.ShapeDtypeStruct((16, 2 * SH), jnp.float32),
            pltpu.HBM((R, 128), jnp.bfloat16),
            jax.ShapeDtypeStruct((R, 128), jnp.float32),
        ),
        in_specs=[pl.BlockSpec(memory_space=pltpu.SMEM)] + [pl.BlockSpec(memory_space=pltpu.VMEM)] * 3,
        out_specs=(
            pl.BlockSpec(memory_space=pltpu.VMEM),
            pl.BlockSpec(memory_space=pltpu.VMEM),
            pl.BlockSpec(memory_space=pltpu.HBM),
            pl.BlockSpec(memory_space=pltpu.VMEM),
        ),
        scratch_shapes=[
            pltpu.VMEM((R, 128), jnp.bfloat16),
            pltpu.VMEM((T1, 128), jnp.float32),
            pltpu.VMEM((T1, 128), jnp.float32),
            pltpu.VMEM((8, C), jnp.float32),
            pltpu.VMEM((8, 2 * SH), jnp.float32),
            pltpu.VMEM((8, 2 * SH), jnp.float32),
            pltpu.SemaphoreType.DMA,
        ],
        compiler_params=pltpu.CompilerParams(vmem_limit_bytes=12 << 20),
    )(own, rows, colsT, colid)


def pack_body(own_ref, keep_ref, got_ref, pay_ref):
    core = own_ref[2]
    mine = keep_ref[...]
    got = got_ref[...]
    low = jnp.where(core == 0, mine[0:8], mine[0:8] + got[0:8])
    high = jnp.where(core == 0, got[0:8], mine[8:16] + got[8:16])
    both = jnp.concatenate([low, high], axis=0)
    for d in range(NB):
        pay_ref[d] = both


def pack(own, keep, got):
    return pl.pallas_call(
        pack_body,
        out_shape=jax.ShapeDtypeStruct((NB, 16, 2 * SH), jnp.float32),
        in_specs=[pl.BlockSpec(memory_space=pltpu.SMEM)] + [pl.BlockSpec(memory_space=pltpu.VMEM)] * 2,
        out_specs=pl.BlockSpec(memory_space=pltpu.VMEM),
        compiler_params=pltpu.CompilerParams(vmem_limit_bytes=6 << 20),
    )(own, keep, got)


def mid_body(own_ref, part_ref, keep_ref, give_ref):
    core = own_ref[2]
    line = own_ref[3]

    def total(lo, hi):
        out = part_ref[lo]
        for d in range(lo + 1, hi):
            out = out + part_ref[d]
        return out

    low = total(0, 8)
    high = total(8, 16)
    rows = low + high
    cols = jnp.where(line == 0, low, high)
    keep_ref[...] = jnp.where(core == 0, rows, cols)
    give_ref[...] = jnp.where(core == 0, jnp.concatenate([rows[8:16], rows[0:8]], axis=0), cols)


def mid(own, part):
    return pl.pallas_call(
        mid_body,
        out_shape=(jax.ShapeDtypeStruct((16, 2 * SH), jnp.float32),) * 2,
        in_specs=[pl.BlockSpec(memory_space=pltpu.SMEM), pl.BlockSpec(memory_space=pltpu.VMEM)],
        out_specs=(pl.BlockSpec(memory_space=pltpu.VMEM),) * 2,
        compiler_params=pltpu.CompilerParams(vmem_limit_bytes=6 << 20),
    )(own, part)


def k2_body(own_ref, rows_in, mates, cols_ref, colsT, colid_ref, keep_ref, got_ref, g_ref, rows, ris, rrow, rcol, sem):
    fetch = pltpu.make_async_copy(rows_in, rows, sem)
    fetch.start()
    b = own_ref[0]
    z = own_ref[1]
    core = own_ref[2]
    mine = keep_ref[...]
    got = got_ref[...]
    by_rows = jnp.where(core == 0, mine, got)
    by_cols = jnp.where(core == 0, got, mine)
    rrow[...] = (1.0 / TAU) / by_rows[0:8]
    tall = by_cols[0:8]
    logs = jnp.sum(jnp.log(tall), axis=0, keepdims=True)
    pos = jnp.sum(by_cols[8:16, 0:128], axis=0, keepdims=True)
    loss = logs[:, 0:128] + logs[:, 128:256] + logs[:, 256:384] - pos * (1.0 / TAU)
    loss = jnp.concatenate([loss, jnp.zeros((7, 128), jnp.float32)], axis=0)
    for d in range(NB):
        g_ref[d, SH : SH + 8, :] = loss
    rcol[8:16, :] = (1.0 / TAU) / tall
    for k in range(NZ):
        rcol[k : k + 1, :] = rcol[pl.ds(8 + ((z + k) & 7), 1), :]

    def tile(t, masked):
        at = pl.multiple_of(t * T2, T2)
        for q in range(0, PER2, 2):
            two = rrow[pl.ds(t * (PER2 // 2) + q // 2, 1), :]
            ris[q * SH : (q + 2) * SH, :] = col_bcast(two)
        u = rows[pl.ds(at, T2), :]
        rid = diag_rows(b, T2) if masked else None
        acc = jnp.zeros((T2, 128), jnp.float32)
        for c in range(NW):
            s = jnp.dot(u, colsT[:, c * CW : (c + 1) * CW], preferred_element_type=jnp.float32)
            blocks = []
            for r in range(0, T2, SUB):
                here = pl.ds(pl.multiple_of(at + r, SUB), SUB)
                m = mates[here, :]
                ri = ris[r : r + SUB, :]
                ws = []
                for l in range(0, CW, 128):
                    p = c * CW + l
                    rj = rcol[p // 384 : p // 384 + 1, p % 384 : p % 384 + 128]
                    w = jnp.exp2(s[r : r + SUB, l : l + 128] * KS) * (ri + rj)
                    w = jnp.where(m == colid_ref[p // 256 : p // 256 + 1, p % 256 : p % 256 + 128], w - 2.0 / TAU, w)
                    if masked and p < 2 * SH:
                        w = jnp.where(diag_of(rid[r : r + SUB], p, core), 0.0, w)
                    ws.append(w.astype(jnp.bfloat16))
                blocks.append(jnp.concatenate(ws, axis=1))
            w = jnp.concatenate(blocks, axis=0)
            acc = acc + jnp.dot(w, cols_ref[c * CW : (c + 1) * CW, :], preferred_element_type=jnp.float32)
        for q in range(PER2):
            g_ref[t * PER2 + q, 0:SH, :] = acc[q * SH : (q + 1) * SH]

    fetch.wait()
    own_tile = b // PER2
    tile(own_tile, True)

    def step(k, _):
        tile((own_tile + k) & (N2 - 1), False)
        return 0

    lax.fori_loop(1, N2, step, 0)


def k2(own, rows, mates, cols, colsT, colid, keep, got):
    return pl.pallas_call(
        k2_body,
        out_shape=jax.ShapeDtypeStruct((NB, SH + 8, 128), jnp.float32),
        in_specs=[pl.BlockSpec(memory_space=pltpu.SMEM), pl.BlockSpec(memory_space=pltpu.HBM)]
        + [pl.BlockSpec(memory_space=pltpu.VMEM)] * 6,
        out_specs=pl.BlockSpec(memory_space=pltpu.VMEM),
        scratch_shapes=[
            pltpu.VMEM((R, 128), jnp.bfloat16),
            pltpu.VMEM((T2, 128), jnp.float32),
            pltpu.VMEM((8, 2 * SH), jnp.float32),
            pltpu.VMEM((16, 2 * SH), jnp.float32),
            pltpu.SemaphoreType.DMA,
        ],
        compiler_params=pltpu.CompilerParams(vmem_limit_bytes=12 << 20),
    )(own, rows, mates, cols, colsT, colid, keep, got)


def inverse_norm(p):
    return lax.rsqrt(jnp.sum(p * p, axis=1, keepdims=True) + EPS)


def prep_body(p_hbm, mate_hbm, pay_ref, low_ref, p_ref, mate_ref, one, sems):
    first = pltpu.make_async_copy(p_hbm, p_ref, sems.at[NB])
    second = pltpu.make_async_copy(mate_hbm, mate_ref, sems.at[NB + 1])
    first.start()
    second.start()
    first.wait()
    second.wait()
    p = p_ref[...]
    low = (p * inverse_norm(p)).astype(jnp.bfloat16)
    m = mate_ref[...].reshape(1, SH)
    m = jnp.concatenate([m[:, 0:128], jnp.concatenate([m[:, 128:], jnp.zeros((1, 64), jnp.int32)], axis=1)], axis=0)
    hi = (m >> 8).astype(jnp.float32)
    lo = (m & 255).astype(jnp.float32)
    code = jnp.concatenate([hi, lo, jnp.zeros((12, 128), jnp.float32)], axis=0).astype(jnp.bfloat16)
    one[0:SH, :] = low
    one[SH:PADR, :] = code
    copies = [pltpu.make_async_copy(one, pay_ref.at[d], sems.at[d]) for d in range(NB)]
    for copy in copies:
        copy.start()
    low_ref[...] = low
    for copy in copies:
        copy.wait()


def prep(p, mate):
    return pl.pallas_call(
        prep_body,
        out_shape=(
            pltpu.HBM((NB, PADR, 128), jnp.bfloat16),
            jax.ShapeDtypeStruct((SH, 128), jnp.bfloat16),
        ),
        in_specs=[pl.BlockSpec(memory_space=pltpu.HBM)] * 2,
        out_specs=(pl.BlockSpec(memory_space=pltpu.HBM), pl.BlockSpec(memory_space=pltpu.VMEM)),
        scratch_shapes=[
            pltpu.VMEM((SH, 128), jnp.float32),
            pltpu.VMEM((SH,), jnp.int32),
            pltpu.VMEM((PADR, 128), jnp.bfloat16),
            pltpu.SemaphoreType.DMA((NB + 2,)),
        ],
        compiler_params=pltpu.CompilerParams(vmem_limit_bytes=6 << 20),
    )(p, mate)


def final_body(p_ref, g_ref, loss_ref, grad_ref):
    p = p_ref[...]
    inv = inverse_norm(p)
    unit = p * inv
    g = g_ref[0]
    for d in range(1, NB):
        g = g + g_ref[d]
    loss_ref[0, 0] = jnp.sum(g[SH:]) / (NA * NB * SH)
    gu = g[:SH]
    inner = jnp.sum(unit * gu, axis=1, keepdims=True)
    grad_ref[...] = inv * (gu - unit * inner)


def final(p, g):
    return pl.pallas_call(
        final_body,
        out_shape=(
            jax.ShapeDtypeStruct((1, 1), jnp.float32),
            jax.ShapeDtypeStruct((SH, 128), jnp.float32),
        ),
        in_specs=[pl.BlockSpec(memory_space=pltpu.VMEM)] * 2,
        out_specs=(pl.BlockSpec(memory_space=pltpu.SMEM), pl.BlockSpec(memory_space=pltpu.VMEM)),
        compiler_params=pltpu.CompilerParams(vmem_limit_bytes=6 << 20),
    )(p, g)


def swap(value):
    return lax.ppermute(value, "c", [(0, 1), (1, 0)])


def seat(z, core):
    z = z % NZ
    return ((z % 4) * 2 + core) * 2 + z // 4


def total_groups():
    def place(x, y, z, core):
        return ((x * 4 + y) * 4 + z % 4) * 4 + core * 2 + z // 4

    planes = [[place(x, y, z, 0) for x in range(4) for y in range(4)] for z in range(NZ)]
    lines = [[place(x, 2 * h + y, z, 1) for y in (0, 1) for z in range(NZ)] for x in range(4) for h in (0, 1)]
    return planes + lines


def along_z(value, k):
    pairs = []
    for z in range(NZ):
        pairs.append((seat(z, 0), seat(z + k, 0)))
        pairs.append((seat(z, 1), seat(z - k, 1)))
    return lax.ppermute(value, ZC, pairs)


def body(projections, partner):
    xy = lax.axis_index(XY)
    z = lax.axis_index(("zh", "zl"))
    core = lax.axis_index("c")
    own = jnp.stack([xy, z, core, lax.axis_index("y") % 2]).astype(jnp.int32)
    pay, low = prep(pltpu.with_memory_space_constraint(projections, pltpu.HBM), pltpu.with_memory_space_constraint(partner, pltpu.HBM))
    rows = lax.all_to_all(pay, XY, 0, 0)
    pair = jnp.stack([low, swap(low)])
    direct = [along_z(pair, k) for k in (1, 2, 3)] + [along_z(low, 4)]
    crossed = [swap(piece) for piece in direct]
    pieces = [pair, *direct[:3], *crossed[:3], direct[3], crossed[3]]
    p = jnp.arange(16 * CH, dtype=jnp.int32)
    zp = (z + p // (2 * SH)) % NZ
    shard = (zp % 4) * 4 + (p // SH % 2) * 2 + zp // 4
    colid = ((xy * NA + shard) * SH + p % SH).astype(jnp.float32).reshape(16, CH)
    pieces = [pltpu.with_memory_space_constraint(piece, pltpu.HBM) for piece in pieces]
    cols, colsT = kcols(own, pieces)
    keep, give, rows, mates = k1(own, rows, colsT, colid)
    part = lax.all_to_all(pack(own, keep, swap(give)), AXES, 0, 0, axis_index_groups=total_groups())
    keep, give = mid(own, part)
    rows = pltpu.with_memory_space_constraint(rows, pltpu.HBM)
    g = k2(own, rows, mates, cols, colsT, colid, keep, swap(give))
    g = lax.all_to_all(g, XY, 0, 0)
    loss, grad = final(projections, g)
    return (loss[0, 0], grad)


def solution(mesh):
    finer = Mesh(mesh.devices.reshape(4, 4, 4, 2, mesh.shape["sub"]), AXES)
    in_specs = (P(AXES, None), P(AXES))
    out_specs = (P(), P(AXES, None))
    return jax.shard_map(body, mesh=finer, in_specs=in_specs, out_specs=out_specs, check_vma=False)
```

```python
import jax
import jax.numpy as jnp
from jax import lax
from jax.experimental import pallas as pl
from jax.experimental.pallas import tpu as pltpu
from jax.sharding import Mesh
from jax.sharding import PartitionSpec as P

AXES = ("x", "y", "zl", "c", "zh")
XY = ("x", "y")
ZC = ("zl", "c", "zh")
EPS = 1e-06
NZ = 8
LOG2E = 1.4426950408889634
TAU = 0.1
KS = LOG2E / TAU
SH = 192
PADR = 208
NB = 16
NA = 16
C = NA * SH
R = NB * SH
CH = 256
T1 = 1536
N1 = R // T1
PER1 = T1 // SH
T2 = 768
N2 = R // T2
PER2 = T2 // SH
NCH = C // CH
SUB = 64
CW = 256
NW = C // CW


def col_bcast(row):
    return jnp.transpose(jnp.broadcast_to(row, (128, row.shape[1])))


def load_rows(rows_ref, rows, mates, s):
    at = pl.multiple_of(s * SH, SH)
    rows[pl.ds(at, SH), :] = rows_ref[s, 0:SH, :]
    code = rows_ref[s, SH:PADR, :].astype(jnp.float32)
    m = code[0:2] * 256.0 + code[2:4]
    mates[pl.ds(at, 128), :] = col_bcast(m[0:1])
    mates[pl.ds(pl.multiple_of(at + 128, 64), 64), :] = col_bcast(m[1:2])[: SH - 128]


def diag_rows(b, count):
    r = lax.broadcasted_iota(jnp.int32, (count, 128), 0) - (b % (count // SH)) * SH
    return jnp.where((r >= 0) & (r < SH), r, -100000)


def diag_of(rid, lane_at, core):
    lanes = lax.broadcasted_iota(jnp.int32, (1, 128), 1) + (lane_at - core * SH)
    return rid == lanes


def kcols_body(own_ref, pair_ref, d1, d2, d3, s1, s2, s3, d4, s4, cols_ref, colsT):
    core = own_ref[2]

    def put(slot, piece):
        cols_ref[pl.ds(pl.multiple_of(slot * SH, SH), SH), :] = piece

    put(8 + core, d4[...])
    put(9 - core, s4[...])
    put(core, pair_ref[0])
    put(1 - core, pair_ref[1])
    for off, ref in ((-1, d1), (-2, d2), (-3, d3), (1, s1), (2, s2), (3, s3)):
        slot = jnp.where(core == 0, off & 7, (-off) & 7) * 2
        first = core if off < 0 else 1 - core
        put(slot + first, ref[0])
        put(slot + 1 - first, ref[1])
    for c in range(NCH):
        colsT[:, c * CH : (c + 1) * CH] = jnp.transpose(cols_ref[c * CH : (c + 1) * CH, :])


def kcols(own, pieces):
    return pl.pallas_call(
        kcols_body,
        out_shape=(
            jax.ShapeDtypeStruct((C, 128), jnp.bfloat16),
            jax.ShapeDtypeStruct((128, C), jnp.bfloat16),
        ),
        in_specs=[pl.BlockSpec(memory_space=pltpu.SMEM)] + [pl.BlockSpec(memory_space=pltpu.VMEM)] * len(pieces),
        out_specs=(pl.BlockSpec(memory_space=pltpu.VMEM),) * 2,
        compiler_params=pltpu.CompilerParams(vmem_limit_bytes=6 << 20),
        cost_estimate=pl.CostEstimate(flops=10**10, transcendentals=0, bytes_accessed=1 << 21),
    )(own, *pieces)


def k1_body(own_ref, rows_ref, colsT, colid_ref, keep_ref, give_ref, rows_out, mates, rows, racc, hval, cacc, tr, tc, sems):
    b = own_ref[0]
    z = own_ref[1]
    core = own_ref[2]
    cacc[...] = jnp.zeros_like(cacc)

    def tile(t, masked):
        at = pl.multiple_of(t * T1, T1)
        for q in range(PER1):
            load_rows(rows_ref, rows, mates, t * PER1 + q)
        u = rows[pl.ds(at, T1), :]
        rid = diag_rows(b, T1) if masked else None
        for c in range(NW):
            s = jnp.dot(u, colsT[:, c * CW : (c + 1) * CW], preferred_element_type=jnp.float32)
            sums = [None] * (CW // 128)
            for r in range(0, T1, SUB):
                m = mates[pl.ds(pl.multiple_of(at + r, SUB), SUB), :]
                ra = None if c == 0 else racc[r : r + SUB, :]
                hv = jnp.zeros((SUB, 128), jnp.float32) if c == 0 else hval[r : r + SUB, :]
                for l in range(0, CW, 128):
                    p = c * CW + l
                    sl = s[r : r + SUB, l : l + 128]
                    el = jnp.exp2(sl * KS)
                    if masked and p < 2 * SH:
                        el = jnp.where(diag_of(rid[r : r + SUB], p, core), 0.0, el)
                    ra = el if ra is None else ra + el
                    hv = jnp.where(m == colid_ref[p // 256 : p // 256 + 1, p % 256 : p % 256 + 128], sl, hv)
                    cs = jnp.sum(el.reshape(SUB // 8, 8, 128), axis=0)
                    sums[l // 128] = cs if r == 0 else sums[l // 128] + cs
                racc[r : r + SUB, :] = ra
                hval[r : r + SUB, :] = hv
            for l in range(0, CW, 128):
                cacc[:, c * CW + l : c * CW + l + 128] += sums[l // 128]
        for q in range(0, PER1, 2):
            part = [jnp.sum(jnp.transpose(racc[k * SH : (k + 1) * SH, :]), axis=0, keepdims=True) for k in (q, q + 1)]
            tr[pl.ds(t * (PER1 // 2) + q // 2, 1), :] = jnp.concatenate(part, axis=1)
        return jnp.sum(hval[...].reshape(T1 // 8, 8, 128), axis=0)

    own_tile = b // PER1
    pos = tile(own_tile, True)

    def step(k, pos):
        return pos + tile((own_tile + k) & (N1 - 1), False)

    pos = lax.fori_loop(1, N1, step, pos)
    keep = pltpu.make_async_copy(rows, rows_out, sems)
    keep.start()
    total = jnp.sum(cacc[...], axis=0, keepdims=True)
    for k in range(NZ):
        tc[pl.ds((z + k) & 7, 1), :] = total[:, k * 2 * SH : (k + 1) * 2 * SH]
    none = jnp.zeros((8, 256), jnp.float32)
    by_rows = jnp.concatenate([tr[...], jnp.zeros((8, 2 * SH), jnp.float32)], axis=0)
    by_cols = jnp.concatenate([tc[...], jnp.concatenate([pos, none], axis=1)], axis=0)
    keep_ref[...] = jnp.where(core == 0, by_rows, by_cols)
    give_ref[...] = jnp.where(core == 0, by_cols, by_rows)
    keep.wait()


def k1(own, rows, colsT, colid):
    return pl.pallas_call(
        k1_body,
        out_shape=(
            jax.ShapeDtypeStruct((16, 2 * SH), jnp.float32),
            jax.ShapeDtypeStruct((16, 2 * SH), jnp.float32),
            pltpu.HBM((R, 128), jnp.bfloat16),
            jax.ShapeDtypeStruct((R, 128), jnp.float32),
        ),
        in_specs=[pl.BlockSpec(memory_space=pltpu.SMEM)] + [pl.BlockSpec(memory_space=pltpu.VMEM)] * 3,
        out_specs=(
            pl.BlockSpec(memory_space=pltpu.VMEM),
            pl.BlockSpec(memory_space=pltpu.VMEM),
            pl.BlockSpec(memory_space=pltpu.HBM),
            pl.BlockSpec(memory_space=pltpu.VMEM),
        ),
        scratch_shapes=[
            pltpu.VMEM((R, 128), jnp.bfloat16),
            pltpu.VMEM((T1, 128), jnp.float32),
            pltpu.VMEM((T1, 128), jnp.float32),
            pltpu.VMEM((8, C), jnp.float32),
            pltpu.VMEM((8, 2 * SH), jnp.float32),
            pltpu.VMEM((8, 2 * SH), jnp.float32),
            pltpu.SemaphoreType.DMA,
        ],
        compiler_params=pltpu.CompilerParams(vmem_limit_bytes=12 << 20),
    )(own, rows, colsT, colid)


def pack_body(own_ref, keep_ref, got_ref, pay_ref):
    core = own_ref[2]
    mine = keep_ref[...]
    got = got_ref[...]
    low = jnp.where(core == 0, mine[0:8], mine[0:8] + got[0:8])
    high = jnp.where(core == 0, got[0:8], mine[8:16] + got[8:16])
    both = jnp.concatenate([low, high], axis=0)
    for d in range(NB):
        pay_ref[d] = both


def pack(own, keep, got):
    return pl.pallas_call(
        pack_body,
        out_shape=jax.ShapeDtypeStruct((NB, 16, 2 * SH), jnp.float32),
        in_specs=[pl.BlockSpec(memory_space=pltpu.SMEM)] + [pl.BlockSpec(memory_space=pltpu.VMEM)] * 2,
        out_specs=pl.BlockSpec(memory_space=pltpu.VMEM),
        compiler_params=pltpu.CompilerParams(vmem_limit_bytes=6 << 20),
    )(own, keep, got)


def mid_body(own_ref, part_ref, keep_ref, give_ref):
    core = own_ref[2]
    line = own_ref[3]

    def total(lo, hi):
        out = part_ref[lo]
        for d in range(lo + 1, hi):
            out = out + part_ref[d]
        return out

    low = total(0, 8)
    high = total(8, 16)
    rows = low + high
    cols = jnp.where(line == 0, low, high)
    keep_ref[...] = jnp.where(core == 0, rows, cols)
    give_ref[...] = jnp.where(core == 0, jnp.concatenate([rows[8:16], rows[0:8]], axis=0), cols)


def mid(own, part):
    return pl.pallas_call(
        mid_body,
        out_shape=(jax.ShapeDtypeStruct((16, 2 * SH), jnp.float32),) * 2,
        in_specs=[pl.BlockSpec(memory_space=pltpu.SMEM), pl.BlockSpec(memory_space=pltpu.VMEM)],
        out_specs=(pl.BlockSpec(memory_space=pltpu.VMEM),) * 2,
        compiler_params=pltpu.CompilerParams(vmem_limit_bytes=6 << 20),
    )(own, part)


def k2_body(own_ref, rows_in, mates, cols_ref, colsT, colid_ref, keep_ref, got_ref, g_ref, rows, ris, rrow, rcol, sem):
    fetch = pltpu.make_async_copy(rows_in, rows, sem)
    fetch.start()
    b = own_ref[0]
    z = own_ref[1]
    core = own_ref[2]
    mine = keep_ref[...]
    got = got_ref[...]
    by_rows = jnp.where(core == 0, mine, got)
    by_cols = jnp.where(core == 0, got, mine)
    rrow[...] = (1.0 / TAU) / by_rows[0:8]
    tall = by_cols[0:8]
    logs = jnp.sum(jnp.log(tall), axis=0, keepdims=True)
    pos = jnp.sum(by_cols[8:16, 0:128], axis=0, keepdims=True)
    loss = logs[:, 0:128] + logs[:, 128:256] + logs[:, 256:384] - pos * (1.0 / TAU)
    loss = jnp.concatenate([loss, jnp.zeros((7, 128), jnp.float32)], axis=0)
    for d in range(NB):
        g_ref[d, SH : SH + 8, :] = loss
    rcol[8:16, :] = (1.0 / TAU) / tall
    for k in range(NZ):
        rcol[k : k + 1, :] = rcol[pl.ds(8 + ((z + k) & 7), 1), :]

    def tile(t, masked):
        at = pl.multiple_of(t * T2, T2)
        for q in range(0, PER2, 2):
            two = rrow[pl.ds(t * (PER2 // 2) + q // 2, 1), :]
            ris[q * SH : (q + 2) * SH, :] = col_bcast(two)
        u = rows[pl.ds(at, T2), :]
        rid = diag_rows(b, T2) if masked else None
        acc = jnp.zeros((T2, 128), jnp.float32)
        for c in range(NW):
            s = jnp.dot(u, colsT[:, c * CW : (c + 1) * CW], preferred_element_type=jnp.float32)
            blocks = []
            for r in range(0, T2, SUB):
                here = pl.ds(pl.multiple_of(at + r, SUB), SUB)
                m = mates[here, :]
                ri = ris[r : r + SUB, :]
                ws = []
                for l in range(0, CW, 128):
                    p = c * CW + l
                    rj = rcol[p // 384 : p // 384 + 1, p % 384 : p % 384 + 128]
                    w = jnp.exp2(s[r : r + SUB, l : l + 128] * KS) * (ri + rj)
                    w = jnp.where(m == colid_ref[p // 256 : p // 256 + 1, p % 256 : p % 256 + 128], w - 2.0 / TAU, w)
                    if masked and p < 2 * SH:
                        w = jnp.where(diag_of(rid[r : r + SUB], p, core), 0.0, w)
                    ws.append(w.astype(jnp.bfloat16))
                blocks.append(jnp.concatenate(ws, axis=1))
            w = jnp.concatenate(blocks, axis=0)
            acc = acc + jnp.dot(w, cols_ref[c * CW : (c + 1) * CW, :], preferred_element_type=jnp.float32)
        for q in range(PER2):
            g_ref[t * PER2 + q, 0:SH, :] = acc[q * SH : (q + 1) * SH]

    fetch.wait()
    own_tile = b // PER2
    tile(own_tile, True)

    def step(k, _):
        tile((own_tile + k) & (N2 - 1), False)
        return 0

    lax.fori_loop(1, N2, step, 0)


def k2(own, rows, mates, cols, colsT, colid, keep, got):
    return pl.pallas_call(
        k2_body,
        out_shape=jax.ShapeDtypeStruct((NB, SH + 8, 128), jnp.float32),
        in_specs=[pl.BlockSpec(memory_space=pltpu.SMEM), pl.BlockSpec(memory_space=pltpu.HBM)]
        + [pl.BlockSpec(memory_space=pltpu.VMEM)] * 6,
        out_specs=pl.BlockSpec(memory_space=pltpu.VMEM),
        scratch_shapes=[
            pltpu.VMEM((R, 128), jnp.bfloat16),
            pltpu.VMEM((T2, 128), jnp.float32),
            pltpu.VMEM((8, 2 * SH), jnp.float32),
            pltpu.VMEM((16, 2 * SH), jnp.float32),
            pltpu.SemaphoreType.DMA,
        ],
        compiler_params=pltpu.CompilerParams(vmem_limit_bytes=12 << 20),
    )(own, rows, mates, cols, colsT, colid, keep, got)


def inverse_norm(p):
    return lax.rsqrt(jnp.sum(p * p, axis=1, keepdims=True) + EPS)


def prep_body(p_hbm, mate_hbm, pay_ref, low_ref, p_ref, mate_ref, one, sems):
    first = pltpu.make_async_copy(p_hbm, p_ref, sems.at[NB])
    second = pltpu.make_async_copy(mate_hbm, mate_ref, sems.at[NB + 1])
    first.start()
    second.start()
    first.wait()
    second.wait()
    p = p_ref[...]
    low = (p * inverse_norm(p)).astype(jnp.bfloat16)
    m = mate_ref[...].reshape(1, SH)
    m = jnp.concatenate([m[:, 0:128], jnp.concatenate([m[:, 128:], jnp.zeros((1, 64), jnp.int32)], axis=1)], axis=0)
    hi = (m >> 8).astype(jnp.float32)
    lo = (m & 255).astype(jnp.float32)
    code = jnp.concatenate([hi, lo, jnp.zeros((12, 128), jnp.float32)], axis=0).astype(jnp.bfloat16)
    one[0:SH, :] = low
    one[SH:PADR, :] = code
    copies = [pltpu.make_async_copy(one, pay_ref.at[d], sems.at[d]) for d in range(NB)]
    for copy in copies:
        copy.start()
    low_ref[...] = low
    for copy in copies:
        copy.wait()


def prep(p, mate):
    return pl.pallas_call(
        prep_body,
        out_shape=(
            pltpu.HBM((NB, PADR, 128), jnp.bfloat16),
            jax.ShapeDtypeStruct((SH, 128), jnp.bfloat16),
        ),
        in_specs=[pl.BlockSpec(memory_space=pltpu.HBM)] * 2,
        out_specs=(pl.BlockSpec(memory_space=pltpu.HBM), pl.BlockSpec(memory_space=pltpu.VMEM)),
        scratch_shapes=[
            pltpu.VMEM((SH, 128), jnp.float32),
            pltpu.VMEM((SH,), jnp.int32),
            pltpu.VMEM((PADR, 128), jnp.bfloat16),
            pltpu.SemaphoreType.DMA((NB + 2,)),
        ],
        compiler_params=pltpu.CompilerParams(vmem_limit_bytes=6 << 20),
    )(p, mate)


def final_body(p_ref, g_ref, loss_ref, grad_ref):
    p = p_ref[...]
    inv = inverse_norm(p)
    unit = p * inv
    g = g_ref[0]
    for d in range(1, NB):
        g = g + g_ref[d]
    loss_ref[0, 0] = jnp.sum(g[SH:]) / (NA * NB * SH)
    gu = g[:SH]
    inner = jnp.sum(unit * gu, axis=1, keepdims=True)
    grad_ref[...] = inv * (gu - unit * inner)


def final(p, g):
    return pl.pallas_call(
        final_body,
        out_shape=(
            jax.ShapeDtypeStruct((1, 1), jnp.float32),
            jax.ShapeDtypeStruct((SH, 128), jnp.float32),
        ),
        in_specs=[pl.BlockSpec(memory_space=pltpu.VMEM)] * 2,
        out_specs=(pl.BlockSpec(memory_space=pltpu.SMEM), pl.BlockSpec(memory_space=pltpu.VMEM)),
        compiler_params=pltpu.CompilerParams(vmem_limit_bytes=6 << 20),
    )(p, g)


def swap(value):
    return lax.ppermute(value, "c", [(0, 1), (1, 0)])


def seat(z, core):
    z = z % NZ
    return ((z % 4) * 2 + core) * 2 + z // 4


def total_groups():
    def place(x, y, z, core):
        return ((x * 4 + y) * 4 + z % 4) * 4 + core * 2 + z // 4

    planes = [[place(x, y, z, 0) for x in range(4) for y in range(4)] for z in range(NZ)]
    lines = [[place(x, 2 * h + y, z, 1) for y in (0, 1) for z in range(NZ)] for x in range(4) for h in (0, 1)]
    return planes + lines


def along_z(value, k):
    pairs = []
    for z in range(NZ):
        pairs.append((seat(z, 0), seat(z + k, 0)))
        pairs.append((seat(z, 1), seat(z - k, 1)))
    return lax.ppermute(value, ZC, pairs)


def body(projections, partner):
    xy = lax.axis_index(XY)
    z = lax.axis_index(("zh", "zl"))
    core = lax.axis_index("c")
    own = jnp.stack([xy, z, core, lax.axis_index("y") % 2]).astype(jnp.int32)
    pay, low = prep(pltpu.with_memory_space_constraint(projections, pltpu.HBM), pltpu.with_memory_space_constraint(partner, pltpu.HBM))
    rows = lax.all_to_all(pay, XY, 0, 0)
    pair = jnp.stack([low, swap(low)])
    direct = [along_z(pair, k) for k in (1, 2, 3)] + [along_z(low, 4)]
    crossed = [swap(piece) for piece in direct]
    pieces = [pair, *direct[:3], *crossed[:3], direct[3], crossed[3]]
    p = jnp.arange(16 * CH, dtype=jnp.int32)
    zp = (z + p // (2 * SH)) % NZ
    shard = (zp % 4) * 4 + (p // SH % 2) * 2 + zp // 4
    colid = ((xy * NA + shard) * SH + p % SH).astype(jnp.float32).reshape(16, CH)
    cols, colsT = kcols(own, pieces)
    keep, give, rows, mates = k1(own, rows, colsT, colid)
    part = lax.all_to_all(pack(own, keep, swap(give)), AXES, 0, 0, axis_index_groups=total_groups())
    keep, give = mid(own, part)
    rows = pltpu.with_memory_space_constraint(rows, pltpu.HBM)
    g = k2(own, rows, mates, cols, colsT, colid, keep, swap(give))
    g = lax.all_to_all(g, XY, 0, 0)
    loss, grad = final(projections, g)
    return (loss[0, 0], grad)


def solution(mesh):
    finer = Mesh(mesh.devices.reshape(4, 4, 4, 2, mesh.shape["sub"]), AXES)
    in_specs = (P(AXES, None), P(AXES))
    out_specs = (P(), P(AXES, None))
    return jax.shard_map(body, mesh=finer, in_specs=in_specs, out_specs=out_specs, check_vma=False)
```

```python
import jax
import jax.numpy as jnp
from jax import lax
from jax.experimental import pallas as pl
from jax.experimental.pallas import tpu as pltpu
from jax.sharding import Mesh
from jax.sharding import PartitionSpec as P

AXES = ("x", "y", "zl", "c", "zh")
XY = ("x", "y")
ZC = ("zl", "c", "zh")
EPS = 1e-06
NZ = 8
LOG2E = 1.4426950408889634
TAU = 0.1
KS = LOG2E / TAU
SH = 192
PADR = 208
NB = 16
NA = 16
C = NA * SH
R = NB * SH
CH = 256
T1 = 1536
N1 = R // T1
PER1 = T1 // SH
T2 = 768
N2 = R // T2
PER2 = T2 // SH
NCH = C // CH
SUB = 64
CW = 256
NW = C // CW


def col_bcast(row):
    return jnp.transpose(jnp.broadcast_to(row, (128, row.shape[1])))


def load_rows(rows_ref, rows, mates, s):
    at = pl.multiple_of(s * SH, SH)
    rows[pl.ds(at, SH), :] = rows_ref[s, 0:SH, :]
    code = rows_ref[s, SH:PADR, :].astype(jnp.float32)
    m = code[0:2] * 256.0 + code[2:4]
    mates[pl.ds(at, 128), :] = col_bcast(m[0:1])
    mates[pl.ds(pl.multiple_of(at + 128, 64), 64), :] = col_bcast(m[1:2])[: SH - 128]


def diag_rows(b, count):
    r = lax.broadcasted_iota(jnp.int32, (count, 128), 0) - (b % (count // SH)) * SH
    return jnp.where((r >= 0) & (r < SH), r, -100000)


def diag_of(rid, lane_at, core):
    lanes = lax.broadcasted_iota(jnp.int32, (1, 128), 1) + (lane_at - core * SH)
    return rid == lanes


def kcols_body(own_ref, pair_ref, d1, d2, d3, s1, s2, s3, d4, s4, cols_ref, colsT):
    core = own_ref[2]

    def put(slot, piece):
        cols_ref[pl.ds(pl.multiple_of(slot * SH, SH), SH), :] = piece

    put(8 + core, d4[...])
    put(9 - core, s4[...])
    put(core, pair_ref[0])
    put(1 - core, pair_ref[1])
    for off, ref in ((-1, d1), (-2, d2), (-3, d3), (1, s1), (2, s2), (3, s3)):
        slot = jnp.where(core == 0, off & 7, (-off) & 7) * 2
        first = core if off < 0 else 1 - core
        put(slot + first, ref[0])
        put(slot + 1 - first, ref[1])
    for c in range(NCH):
        colsT[:, c * CH : (c + 1) * CH] = jnp.transpose(cols_ref[c * CH : (c + 1) * CH, :])


def kcols(own, pieces):
    return pl.pallas_call(
        kcols_body,
        out_shape=(
            jax.ShapeDtypeStruct((C, 128), jnp.bfloat16),
            jax.ShapeDtypeStruct((128, C), jnp.bfloat16),
        ),
        in_specs=[pl.BlockSpec(memory_space=pltpu.SMEM)] + [pl.BlockSpec(memory_space=pltpu.VMEM)] * len(pieces),
        out_specs=(pl.BlockSpec(memory_space=pltpu.VMEM),) * 2,
        compiler_params=pltpu.CompilerParams(vmem_limit_bytes=6 << 20),
        cost_estimate=pl.CostEstimate(flops=10**10, transcendentals=0, bytes_accessed=1 << 21),
    )(own, *pieces)


def k1_body(own_ref, rows_ref, colsT, colid_ref, keep_ref, give_ref, rows, mates, racc, hval, cacc, tr, tc):
    b = own_ref[0]
    z = own_ref[1]
    core = own_ref[2]
    cacc[...] = jnp.zeros_like(cacc)

    def tile(t, masked):
        at = pl.multiple_of(t * T1, T1)
        for q in range(PER1):
            load_rows(rows_ref, rows, mates, t * PER1 + q)
        u = rows[pl.ds(at, T1), :]
        rid = diag_rows(b, T1) if masked else None
        for c in range(NW):
            s = jnp.dot(u, colsT[:, c * CW : (c + 1) * CW], preferred_element_type=jnp.float32)
            sums = [None] * (CW // 128)
            for r in range(0, T1, SUB):
                m = mates[pl.ds(pl.multiple_of(at + r, SUB), SUB), :]
                ra = None if c == 0 else racc[r : r + SUB, :]
                hv = jnp.zeros((SUB, 128), jnp.float32) if c == 0 else hval[r : r + SUB, :]
                for l in range(0, CW, 128):
                    p = c * CW + l
                    sl = s[r : r + SUB, l : l + 128]
                    el = jnp.exp2(sl * KS)
                    if masked and p < 2 * SH:
                        el = jnp.where(diag_of(rid[r : r + SUB], p, core), 0.0, el)
                    ra = el if ra is None else ra + el
                    hv = jnp.where(m == colid_ref[p // 256 : p // 256 + 1, p % 256 : p % 256 + 128], sl, hv)
                    cs = jnp.sum(el.reshape(SUB // 8, 8, 128), axis=0)
                    sums[l // 128] = cs if r == 0 else sums[l // 128] + cs
                racc[r : r + SUB, :] = ra
                hval[r : r + SUB, :] = hv
            for l in range(0, CW, 128):
                cacc[:, c * CW + l : c * CW + l + 128] += sums[l // 128]
        for q in range(0, PER1, 2):
            part = [jnp.sum(jnp.transpose(racc[k * SH : (k + 1) * SH, :]), axis=0, keepdims=True) for k in (q, q + 1)]
            tr[pl.ds(t * (PER1 // 2) + q // 2, 1), :] = jnp.concatenate(part, axis=1)
        return jnp.sum(hval[...].reshape(T1 // 8, 8, 128), axis=0)

    own_tile = b // PER1
    pos = tile(own_tile, True)

    def step(k, pos):
        return pos + tile((own_tile + k) & (N1 - 1), False)

    pos = lax.fori_loop(1, N1, step, pos)
    total = jnp.sum(cacc[...], axis=0, keepdims=True)
    for k in range(NZ):
        tc[pl.ds((z + k) & 7, 1), :] = total[:, k * 2 * SH : (k + 1) * 2 * SH]
    none = jnp.zeros((8, 256), jnp.float32)
    by_rows = jnp.concatenate([tr[...], jnp.zeros((8, 2 * SH), jnp.float32)], axis=0)
    by_cols = jnp.concatenate([tc[...], jnp.concatenate([pos, none], axis=1)], axis=0)
    keep_ref[...] = jnp.where(core == 0, by_rows, by_cols)
    give_ref[...] = jnp.where(core == 0, by_cols, by_rows)


def k1(own, rows, colsT, colid):
    return pl.pallas_call(
        k1_body,
        out_shape=(
            jax.ShapeDtypeStruct((16, 2 * SH), jnp.float32),
            jax.ShapeDtypeStruct((16, 2 * SH), jnp.float32),
            jax.ShapeDtypeStruct((R, 128), jnp.bfloat16),
            jax.ShapeDtypeStruct((R, 128), jnp.float32),
        ),
        in_specs=[pl.BlockSpec(memory_space=pltpu.SMEM)] + [pl.BlockSpec(memory_space=pltpu.VMEM)] * 3,
        out_specs=(
            pl.BlockSpec(memory_space=pltpu.VMEM),
            pl.BlockSpec(memory_space=pltpu.VMEM),
            pl.BlockSpec(memory_space=pltpu.VMEM),
            pl.BlockSpec(memory_space=pltpu.VMEM),
        ),
        scratch_shapes=[
            pltpu.VMEM((T1, 128), jnp.float32),
            pltpu.VMEM((T1, 128), jnp.float32),
            pltpu.VMEM((8, C), jnp.float32),
            pltpu.VMEM((8, 2 * SH), jnp.float32),
            pltpu.VMEM((8, 2 * SH), jnp.float32),
        ],
        compiler_params=pltpu.CompilerParams(vmem_limit_bytes=12 << 20),
    )(own, rows, colsT, colid)


def pack_body(own_ref, keep_ref, got_ref, pay_ref):
    core = own_ref[2]
    mine = keep_ref[...]
    got = got_ref[...]
    low = jnp.where(core == 0, mine[0:8], mine[0:8] + got[0:8])
    high = jnp.where(core == 0, got[0:8], mine[8:16] + got[8:16])
    both = jnp.concatenate([low, high], axis=0)
    for d in range(NB):
        pay_ref[d] = both


def pack(own, keep, got):
    return pl.pallas_call(
        pack_body,
        out_shape=jax.ShapeDtypeStruct((NB, 16, 2 * SH), jnp.float32),
        in_specs=[pl.BlockSpec(memory_space=pltpu.SMEM)] + [pl.BlockSpec(memory_space=pltpu.VMEM)] * 2,
        out_specs=pl.BlockSpec(memory_space=pltpu.VMEM),
        compiler_params=pltpu.CompilerParams(vmem_limit_bytes=6 << 20),
    )(own, keep, got)


def mid_body(own_ref, part_ref, keep_ref, give_ref):
    core = own_ref[2]
    line = own_ref[3]

    def total(lo, hi):
        out = part_ref[lo]
        for d in range(lo + 1, hi):
            out = out + part_ref[d]
        return out

    low = total(0, 8)
    high = total(8, 16)
    rows = low + high
    cols = jnp.where(line == 0, low, high)
    keep_ref[...] = jnp.where(core == 0, rows, cols)
    give_ref[...] = jnp.where(core == 0, jnp.concatenate([rows[8:16], rows[0:8]], axis=0), cols)


def mid(own, part):
    return pl.pallas_call(
        mid_body,
        out_shape=(jax.ShapeDtypeStruct((16, 2 * SH), jnp.float32),) * 2,
        in_specs=[pl.BlockSpec(memory_space=pltpu.SMEM), pl.BlockSpec(memory_space=pltpu.VMEM)],
        out_specs=(pl.BlockSpec(memory_space=pltpu.VMEM),) * 2,
        compiler_params=pltpu.CompilerParams(vmem_limit_bytes=6 << 20),
    )(own, part)


def k2_body(own_ref, rows, mates, cols_ref, colsT, colid_ref, keep_ref, got_ref, g_ref, ris, rrow, rcol):
    b = own_ref[0]
    z = own_ref[1]
    core = own_ref[2]
    mine = keep_ref[...]
    got = got_ref[...]
    by_rows = jnp.where(core == 0, mine, got)
    by_cols = jnp.where(core == 0, got, mine)
    rrow[...] = (1.0 / TAU) / by_rows[0:8]
    tall = by_cols[0:8]
    logs = jnp.sum(jnp.log(tall), axis=0, keepdims=True)
    pos = jnp.sum(by_cols[8:16, 0:128], axis=0, keepdims=True)
    loss = logs[:, 0:128] + logs[:, 128:256] + logs[:, 256:384] - pos * (1.0 / TAU)
    loss = jnp.concatenate([loss, jnp.zeros((7, 128), jnp.float32)], axis=0)
    for d in range(NB):
        g_ref[d, SH : SH + 8, :] = loss
    rcol[8:16, :] = (1.0 / TAU) / tall
    for k in range(NZ):
        rcol[k : k + 1, :] = rcol[pl.ds(8 + ((z + k) & 7), 1), :]

    def tile(t, masked):
        at = pl.multiple_of(t * T2, T2)
        for q in range(0, PER2, 2):
            two = rrow[pl.ds(t * (PER2 // 2) + q // 2, 1), :]
            ris[q * SH : (q + 2) * SH, :] = col_bcast(two)
        u = rows[pl.ds(at, T2), :]
        rid = diag_rows(b, T2) if masked else None
        acc = jnp.zeros((T2, 128), jnp.float32)
        for c in range(NW):
            s = jnp.dot(u, colsT[:, c * CW : (c + 1) * CW], preferred_element_type=jnp.float32)
            blocks = []
            for r in range(0, T2, SUB):
                here = pl.ds(pl.multiple_of(at + r, SUB), SUB)
                m = mates[here, :]
                ri = ris[r : r + SUB, :]
                ws = []
                for l in range(0, CW, 128):
                    p = c * CW + l
                    rj = rcol[p // 384 : p // 384 + 1, p % 384 : p % 384 + 128]
                    w = jnp.exp2(s[r : r + SUB, l : l + 128] * KS) * (ri + rj)
                    w = jnp.where(m == colid_ref[p // 256 : p // 256 + 1, p % 256 : p % 256 + 128], w - 2.0 / TAU, w)
                    if masked and p < 2 * SH:
                        w = jnp.where(diag_of(rid[r : r + SUB], p, core), 0.0, w)
                    ws.append(w.astype(jnp.bfloat16))
                blocks.append(jnp.concatenate(ws, axis=1))
            w = jnp.concatenate(blocks, axis=0)
            acc = acc + jnp.dot(w, cols_ref[c * CW : (c + 1) * CW, :], preferred_element_type=jnp.float32)
        for q in range(PER2):
            g_ref[t * PER2 + q, 0:SH, :] = acc[q * SH : (q + 1) * SH]

    own_tile = b // PER2
    tile(own_tile, True)

    def step(k, _):
        tile((own_tile + k) & (N2 - 1), False)
        return 0

    lax.fori_loop(1, N2, step, 0)


def k2(own, rows, mates, cols, colsT, colid, keep, got):
    return pl.pallas_call(
        k2_body,
        out_shape=jax.ShapeDtypeStruct((NB, SH + 8, 128), jnp.float32),
        in_specs=[pl.BlockSpec(memory_space=pltpu.SMEM)] + [pl.BlockSpec(memory_space=pltpu.VMEM)] * 7,
        out_specs=pl.BlockSpec(memory_space=pltpu.VMEM),
        scratch_shapes=[
            pltpu.VMEM((T2, 128), jnp.float32),
            pltpu.VMEM((8, 2 * SH), jnp.float32),
            pltpu.VMEM((16, 2 * SH), jnp.float32),
        ],
        compiler_params=pltpu.CompilerParams(vmem_limit_bytes=12 << 20),
    )(own, rows, mates, cols, colsT, colid, keep, got)


def inverse_norm(p):
    return lax.rsqrt(jnp.sum(p * p, axis=1, keepdims=True) + EPS)


def prep_body(p_hbm, mate_hbm, pay_ref, low_ref, p_ref, mate_ref, one, sems):
    first = pltpu.make_async_copy(p_hbm, p_ref, sems.at[NB])
    second = pltpu.make_async_copy(mate_hbm, mate_ref, sems.at[NB + 1])
    first.start()
    second.start()
    first.wait()
    second.wait()
    p = p_ref[...]
    low = (p * inverse_norm(p)).astype(jnp.bfloat16)
    m = mate_ref[...].reshape(1, SH)
    m = jnp.concatenate([m[:, 0:128], jnp.concatenate([m[:, 128:], jnp.zeros((1, 64), jnp.int32)], axis=1)], axis=0)
    hi = (m >> 8).astype(jnp.float32)
    lo = (m & 255).astype(jnp.float32)
    code = jnp.concatenate([hi, lo, jnp.zeros((12, 128), jnp.float32)], axis=0).astype(jnp.bfloat16)
    one[0:SH, :] = low
    one[SH:PADR, :] = code
    copies = [pltpu.make_async_copy(one, pay_ref.at[d], sems.at[d]) for d in range(NB)]
    for copy in copies:
        copy.start()
    low_ref[...] = low
    for copy in copies:
        copy.wait()


def prep(p, mate):
    return pl.pallas_call(
        prep_body,
        out_shape=(
            pltpu.HBM((NB, PADR, 128), jnp.bfloat16),
            jax.ShapeDtypeStruct((SH, 128), jnp.bfloat16),
        ),
        in_specs=[pl.BlockSpec(memory_space=pltpu.HBM)] * 2,
        out_specs=(pl.BlockSpec(memory_space=pltpu.HBM), pl.BlockSpec(memory_space=pltpu.VMEM)),
        scratch_shapes=[
            pltpu.VMEM((SH, 128), jnp.float32),
            pltpu.VMEM((SH,), jnp.int32),
            pltpu.VMEM((PADR, 128), jnp.bfloat16),
            pltpu.SemaphoreType.DMA((NB + 2,)),
        ],
        compiler_params=pltpu.CompilerParams(vmem_limit_bytes=6 << 20),
    )(p, mate)


def final_body(p_ref, g_ref, loss_ref, grad_ref):
    p = p_ref[...]
    inv = inverse_norm(p)
    unit = p * inv
    g = g_ref[0]
    for d in range(1, NB):
        g = g + g_ref[d]
    loss_ref[0, 0] = jnp.sum(g[SH:]) / (NA * NB * SH)
    gu = g[:SH]
    inner = jnp.sum(unit * gu, axis=1, keepdims=True)
    grad_ref[...] = inv * (gu - unit * inner)


def final(p, g):
    return pl.pallas_call(
        final_body,
        out_shape=(
            jax.ShapeDtypeStruct((1, 1), jnp.float32),
            jax.ShapeDtypeStruct((SH, 128), jnp.float32),
        ),
        in_specs=[pl.BlockSpec(memory_space=pltpu.VMEM)] * 2,
        out_specs=(pl.BlockSpec(memory_space=pltpu.SMEM), pl.BlockSpec(memory_space=pltpu.VMEM)),
        compiler_params=pltpu.CompilerParams(vmem_limit_bytes=6 << 20),
    )(p, g)


def swap(value):
    return lax.ppermute(value, "c", [(0, 1), (1, 0)])


def seat(z, core):
    z = z % NZ
    return ((z % 4) * 2 + core) * 2 + z // 4


def total_groups():
    def place(x, y, z, core):
        return ((x * 4 + y) * 4 + z % 4) * 4 + core * 2 + z // 4

    planes = [[place(x, y, z, 0) for x in range(4) for y in range(4)] for z in range(NZ)]
    lines = [[place(x, 2 * h + y, z, 1) for y in (0, 1) for z in range(NZ)] for x in range(4) for h in (0, 1)]
    return planes + lines


def along_z(value, k):
    pairs = []
    for z in range(NZ):
        pairs.append((seat(z, 0), seat(z + k, 0)))
        pairs.append((seat(z, 1), seat(z - k, 1)))
    return lax.ppermute(value, ZC, pairs)


def body(projections, partner):
    xy = lax.axis_index(XY)
    z = lax.axis_index(("zh", "zl"))
    core = lax.axis_index("c")
    own = jnp.stack([xy, z, core, lax.axis_index("y") % 2]).astype(jnp.int32)
    pay, low = prep(pltpu.with_memory_space_constraint(projections, pltpu.HBM), pltpu.with_memory_space_constraint(partner, pltpu.HBM))
    rows = lax.all_to_all(pay, XY, 0, 0)
    pair = jnp.stack([low, swap(low)])
    direct = [along_z(pair, k) for k in (1, 2, 3)] + [along_z(low, 4)]
    crossed = [swap(piece) for piece in direct]
    pieces = [pair, *direct[:3], *crossed[:3], direct[3], crossed[3]]
    p = jnp.arange(16 * CH, dtype=jnp.int32)
    zp = (z + p // (2 * SH)) % NZ
    shard = (zp % 4) * 4 + (p // SH % 2) * 2 + zp // 4
    colid = ((xy * NA + shard) * SH + p % SH).astype(jnp.float32).reshape(16, CH)
    cols, colsT = kcols(own, pieces)
    keep, give, rows, mates = k1(own, rows, colsT, colid)
    part = lax.all_to_all(pack(own, keep, swap(give)), AXES, 0, 0, axis_index_groups=total_groups())
    keep, give = mid(own, part)
    g = k2(own, rows, mates, cols, colsT, colid, keep, swap(give))
    g = lax.all_to_all(g, XY, 0, 0)
    loss, grad = final(projections, g)
    return (loss[0, 0], grad)


def solution(mesh):
    finer = Mesh(mesh.devices.reshape(4, 4, 4, 2, mesh.shape["sub"]), AXES)
    in_specs = (P(AXES, None), P(AXES))
    out_specs = (P(), P(AXES, None))
    return jax.shard_map(body, mesh=finer, in_specs=in_specs, out_specs=out_specs, check_vma=False)
```
